256 devices in a mesh: outer: 16 (over y_hi, x, core), inner: 16 (over y_lo, z).
Axes of the slice: x: 4, y: 4 (y_hi: 2, y_lo: 2; y = y_hi * 2 + y_lo), z: 8, core: 2. Of those that a mesh axis runs over, the one named last changes fastest.
Arguments:
- projected: bfloat16 [32768, 12288], P(('outer', 'inner')), may hold values from -6 to 6
- short_taps: float32 [3, 12288], replicated, may hold values from -3 to 3
- rates: float32 [4096, 16], replicated, may hold values from 7.6293945e-06 to 0.05
- residues: float32 [4096, 16], replicated, may hold values from -1.5 to 1.5
- skip_gain: float32 [4096], replicated, may hold values from -4 to 4
Outputs:
- gated: bfloat16 [32768, 4096], P(('outer', 'inner'))
The draws below stay inside these ranges and needn't reach their ends.
All inputs are finite; a program needn't handle non-finite values.
Results may differ from the reference program's by a relative error of at most 0.008.
Values may be sent and summed in bfloat16 or wider, within the bound.
A program may use at most 128 MiB of HBM per device.

```python
import math
import jax
import jax.numpy as jnp

CH = 4096
MODES = 16
TOKENS = 32768


def shard_levels(key, extent, pieces, least, largest):
    level, own = 1.0, jax.random.fold_in(key, 6)
    for dim, shards_of in pieces:
        draws = jnp.exp(jax.random.uniform(jax.random.fold_in(own, dim), (shards_of,), jnp.float32, least / len(pieces), largest / len(pieces)))
        level = level * jnp.repeat(draws, extent[dim] // shards_of).reshape([-1 if axis == dim else 1 for axis in range(len(extent))])
    return level


def normal_values(stream_key, shape, deviation, reach, pieces=(), dtype=jnp.bfloat16):
    values = deviation * jax.random.normal(stream_key, shape, jnp.float32)
    if pieces:
        values = values * shard_levels(stream_key, shape, pieces, -0.22, 0.18)
    return jnp.clip(values, -reach, reach).astype(dtype)


def setup_inputs(seed: int = 0) -> dict:
    arg_keys = jax.random.split(jax.random.key(seed), 6)
    return {
        "projected": normal_values(arg_keys[0], (TOKENS, 3 * CH), 1.0, 6.0, ((0, 256),)),
        "short_taps": normal_values(arg_keys[1], (3, 3 * CH), 0.5, 3.0, (), jnp.float32),
        "rates": jnp.clip(jnp.exp(jax.random.uniform(arg_keys[2], (CH, MODES), jnp.float32, math.log(7.62939453125e-06), math.log(0.05))), 7.62939453125e-06, 0.05),
        "residues": normal_values(arg_keys[3], (CH, MODES), MODES ** -0.5, 1.5, (), jnp.float32),
        "skip_gain": normal_values(arg_keys[4], (CH,), 1.0, 4.0, (), jnp.float32),
    }


def reference(projected, short_taps, rates, residues, skip_gain):
    padded = jnp.concatenate([jnp.zeros((2, 3 * CH), jnp.bfloat16), projected], 0).astype(jnp.float32)
    feat = short_taps[0] * padded[2:] + short_taps[1] * padded[1:-1] + short_taps[2] * padded[:-2]
    query = feat[:, :CH]
    key_part = feat[:, CH:2 * CH]
    value = feat[:, 2 * CH:]
    mixed = key_part * value
    times = jnp.arange(TOKENS).astype(jnp.float32)
    filt = jnp.zeros((TOKENS, CH), jnp.float32)
    for mode in range(MODES):
        amplitude = residues[:, mode] * jnp.sqrt(2.0 * rates[:, mode])
        filt = filt + amplitude[None, :] * jnp.exp(-rates[:, mode][None, :] * times[:, None])
    spec_mixed = jnp.fft.rfft(mixed, n=2 * TOKENS, axis=0)
    spec_filt = jnp.fft.rfft(filt, n=2 * TOKENS, axis=0)
    conv = jnp.fft.irfft(spec_mixed * spec_filt, n=2 * TOKENS, axis=0)[:TOKENS]
    return (query * (conv + skip_gain[None, :] * mixed)).astype(jnp.bfloat16)
```

```python
import functools

import jax
import jax.numpy as jnp
from jax import lax
from jax.experimental import pallas as pl
from jax.experimental.pallas import tpu as pltpu
from jax.sharding import PartitionSpec as P

MESH = pl.DeviceIdType.MESH
F32 = jnp.float32
BF16 = jnp.bfloat16
SUB = 8
LANE = 128
GROUP = SUB * LANE
CHUNK = 16


def kernel(dims, proj, taps_in, rates_in, resid_in, skip_in, out, raw, ktm, vtm, qtm, base, taps_n, rate_n, res_n,
           skip_v, taps_t, rtm, dtm, atm, zfin, edge, stg, ctm, hsend, hrecv, send1, recv1, send2, recv2, send3, recv3,
           outb, in_sem, par_sem, out_sem, hs_sem, hr_sem, s1_sem, r1_sem, s2_sem, r2_sem, s3_sem, r3_sem):
    outer_n, inner_n, rows, channels, modes = dims
    groups = channels // GROUP
    chunks = rows // CHUNK
    per_owner = channels // inner_n
    owners_g = GROUP // per_owner
    block = modes * per_owner // LANE
    sub_o = per_owner // LANE
    last = rows - CHUNK
    o = lax.axis_index("outer")
    i = lax.axis_index("inner")
    p = o * inner_n + i
    total = outer_n * inner_n
    nxt, prv = lax.rem(p + 1, total), lax.rem(p + total - 1, total)
    nxt_id = (nxt // inner_n, lax.rem(nxt, inner_n))
    prv_id = (prv // inner_n, lax.rem(prv, inner_n))

    bar = pltpu.get_barrier_semaphore()
    for k in range(1, inner_n):
        pl.semaphore_signal(bar, inc=1, device_id=(o, lax.rem(i + k, inner_n)), device_id_type=MESH)
    for k in range(1, outer_n):
        pl.semaphore_signal(bar, inc=1, device_id=(lax.rem(o + k, outer_n), i), device_id_type=MESH)
    pl.semaphore_signal(bar, inc=1, device_id=nxt_id, device_id_type=MESH)
    pl.semaphore_signal(bar, inc=1, device_id=prv_id, device_id_type=MESH)

    tail_cp = pltpu.make_async_copy(proj.at[pl.ds(last, CHUNK), :], raw.at[pl.ds(last, CHUNK), :], in_sem.at[3 * groups])
    tail_cp.start()
    par_cps = [pltpu.make_async_copy(a, b, par_sem.at[n]) for n, (a, b) in enumerate(
        ((taps_in, taps_n), (rates_in, rate_n), (resid_in, res_n), (skip_in, skip_v)))]
    for cp in par_cps:
        cp.start()

    def in_copy(f, g):
        cols = pl.ds((f * groups + g) * GROUP, GROUP)
        return pltpu.make_async_copy(proj.at[pl.ds(0, last), cols], raw.at[pl.ds(0, last), cols],
                                     in_sem.at[f * groups + g])

    for g in range(groups):
        in_copy(1, g).start()
        in_copy(2, g).start()
    for g in range(groups):
        in_copy(0, g).start()
    tms = (qtm, ktm, vtm)

    def relay_chunk(f, g, c):
        for s in range(SUB):
            col = (f * groups + g) * GROUP + s * LANE
            v = raw[pl.ds(pl.multiple_of(c * CHUNK, CHUNK), CHUNK), pl.ds(col, LANE)].astype(F32)
            tms[f][g, pl.ds(c * (CHUNK * SUB) + s, CHUNK, stride=SUB), :] = v

    tail_cp.wait()
    for f in range(3):
        for g in range(groups):
            relay_chunk(f, g, chunks - 1)
            hsend[f * groups + g] = tms[f][g, pl.ds((rows - 2) * SUB, 2 * SUB), :].astype(BF16)

    for cp in par_cps:
        cp.wait()
    for fg in range(3 * groups):
        for s in range(SUB):
            taps_t[pl.ds(fg * 3 * SUB + s, 3, stride=SUB), :] = taps_n[:, pl.ds(fg * GROUP + s * LANE, LANE)]
    for g in range(groups):
        for s in range(SUB):
            cols = pl.ds(g * GROUP + s * LANE, LANE)
            r = rate_n[:, cols]
            rtm[g, pl.ds(s, modes, stride=SUB), :] = r
            dtm[g, pl.ds(s, modes, stride=SUB), :] = jnp.exp(-r)
            atm[g, pl.ds(s, modes, stride=SUB), :] = res_n[:, cols] * jnp.sqrt(2.0 * r)

    def tap(f, g):
        return [taps_t[pl.ds(((f * groups + g) * 3 + j) * SUB, SUB), :] for j in range(3)]

    def mode(ref, g, m):
        return ref[g, pl.ds(m * SUB, SUB), :]

    def tok(ref, g, t):
        return ref[g, pl.ds(pl.multiple_of(t * SUB, SUB), SUB), :]

    def tree(vals):
        vals = list(vals)
        while len(vals) > 1:
            vals = [a + b for a, b in zip(vals[::2], vals[1::2])] + (vals[-1:] if len(vals) % 2 else [])
        return vals[0]

    def recur(g):
        d = [mode(dtm, g, m) for m in range(modes)]
        tk, tv = tap(1, g), tap(2, g)
        sk = skip_v[pl.ds(g * SUB, SUB), :]

        def body(t2, carry):
            z = list(carry[:modes])
            k1, k2, v1, v2 = carry[modes:]
            xs = []
            for u in range(2):
                k0, v0 = tok(ktm, g, t2 * 2 + u), tok(vtm, g, t2 * 2 + u)
                xs.append((tk[0] * k0 + tk[1] * k1 + tk[2] * k2) * (tv[0] * v0 + tv[1] * v1 + tv[2] * v2))
                k1, k2, v1, v2 = k0, k1, v0, v1
            accs = [[xs[0] * sk, None, None, None], [xs[1] * sk, None, None, None]]
            for m in range(modes):
                a = mode(atm, g, m)
                for u in range(2):
                    z[m] = d[m] * z[m] + xs[u]
                    term = a * z[m]
                    old = accs[u][m % 4]
                    accs[u][m % 4] = term if old is None else old + term
            for u in range(2):
                base[g, pl.ds(pl.multiple_of((t2 * 2 + u) * SUB, SUB), SUB), :] = tree(accs[u])
            return (*z, k1, k2, v1, v2)

        zero = jnp.zeros((SUB, LANE), F32)
        init = (*([zero] * modes), tok(ktm, g, 1), tok(ktm, g, 0), tok(vtm, g, 1), tok(vtm, g, 0))
        done = lax.fori_loop(1, rows // 2, body, init)
        for m in range(modes):
            zfin[g, pl.ds(m * SUB, SUB), :] = done[m]

    halo = pltpu.make_async_remote_copy(src_ref=hsend, dst_ref=hrecv, send_sem=hs_sem, recv_sem=hr_sem,
                                        device_id=nxt_id, device_id_type=MESH)
    for g in range(groups):
        if g == groups // 2:
            pl.semaphore_wait(bar, inner_n + outer_n)
            halo.start()
        for f in (1, 2):
            in_copy(f, g).wait()

        def relay(c, _):
            relay_chunk(1, g, c)
            relay_chunk(2, g, c)
            return 0

        lax.fori_loop(0, chunks - 1, relay, 0)
        recur(g)

    halo.wait_recv()
    first = p == 0

    def halo_of(f, g):
        both = hrecv[f * groups + g].astype(F32)
        both = jnp.where(first, jnp.zeros_like(both), both)
        return both[:SUB], both[SUB:]

    for g in range(groups):
        feats = []
        for f in (1, 2):
            h2, h1 = halo_of(f, g)
            t0, t1, t2 = tap(f, g)
            e0, e1 = tok(tms[f], g, 0), tok(tms[f], g, 1)
            feats.append((t0 * e0 + t1 * h1 + t2 * h2, t0 * e1 + t1 * e0 + t2 * h1))
        x0, x1 = feats[0][0] * feats[1][0], feats[0][1] * feats[1][1]
        edge[g, pl.ds(0, SUB), :] = x0
        edge[g, pl.ds(SUB, SUB), :] = x1
        for m in range(modes):
            state = mode(zfin, g, m) + jnp.exp(-(rows - 2.0) * mode(rtm, g, m)) * (mode(dtm, g, m) * x0 + x1)
            stg[g, pl.ds(m, SUB, stride=modes), :] = state
        for w in range(owners_g):
            j = g * owners_g + w
            val = stg[g, pl.ds(w * block, block), :].astype(BF16)

            @pl.when(j == i)
            def _():
                recv1[j] = val

            @pl.when(j != i)
            def _():
                send1[j] = val
                pltpu.make_async_remote_copy(src_ref=send1.at[j], dst_ref=recv1.at[i], send_sem=s1_sem.at[j],
                                             recv_sem=r1_sem.at[i], device_id=(o, j), device_id_type=MESH).start()

    for g in range(groups):
        in_copy(0, g).wait()

        def relay_q(c, _):
            relay_chunk(0, g, c)
            return 0

        lax.fori_loop(0, chunks - 1, relay_q, 0)
        t0, t1, t2 = tap(0, g)
        h2, h1 = halo_of(0, g)

        def gate(t, carry):
            q1, q2 = carry
            for u in range(2):
                q0 = tok(qtm, g, t * 2 + u)
                qtm[g, pl.ds(pl.multiple_of((t * 2 + u) * SUB, SUB), SUB), :] = t0 * q0 + t1 * q1 + t2 * q2
                q1, q2 = q0, q1
            return q1, q2

        lax.fori_loop(0, rows // 2, gate, (h1, h2))

    for n in range(inner_n):
        @pl.when(n != i)
        def _():
            pltpu.make_async_remote_copy(src_ref=send1.at[n], dst_ref=recv1.at[n], send_sem=s1_sem.at[n],
                                         recv_sem=r1_sem.at[n], device_id=(o, n), device_id_type=MESH).wait_recv()

    def own_rate(w):
        return rate_n[:, pl.ds(pl.multiple_of(i * per_owner + w * LANE, LANE), LANE)]

    own = jnp.concatenate([own_rate(w) for w in range(sub_o)], axis=0)
    dec_in = jnp.exp(-float(rows) * own)
    dec_out = jnp.exp(-float(rows * inner_n) * own)
    run = recv1[0].astype(F32)
    for n in range(1, inner_n):
        run = dec_in * run + recv1[n].astype(F32)
    send2[...] = run.astype(BF16)
    for k in range(1, outer_n):
        @pl.when(o + k < outer_n)
        def _():
            pltpu.make_async_remote_copy(src_ref=send2, dst_ref=recv2.at[o], send_sem=s2_sem.at[k],
                                         recv_sem=r2_sem.at[o], device_id=(o + k, i), device_id_type=MESH).start()

    for g in range(groups):
        x0, x1 = edge[g, pl.ds(0, SUB), :], edge[g, pl.ds(SUB, SUB), :]
        sk = skip_v[pl.ds(g * SUB, SUB), :]
        lead = tree([mode(atm, g, m) * jnp.exp(mode(rtm, g, m)) for m in range(modes)])
        base[g, pl.ds(0, SUB), :] = sk * x0 - x1 * lead
        base[g, pl.ds(SUB, SUB), :] = sk * x1
        for m in range(modes):
            r = mode(rtm, g, m)
            zfin[g, pl.ds(m * SUB, SUB), :] = jnp.exp(r) * x0 + jnp.exp(2.0 * r) * x1

    def add_outer(n, acc):
        pltpu.make_async_remote_copy(src_ref=send2, dst_ref=recv2.at[n], send_sem=s2_sem.at[0],
                                     recv_sem=r2_sem.at[n], device_id=(n, i), device_id_type=MESH).wait_recv()
        return dec_out * acc + recv2[n].astype(F32)

    run = lax.fori_loop(0, o, add_outer, jnp.zeros((block, LANE), F32))
    for n in range(inner_n):
        send3[n] = run.astype(BF16)
        if n < inner_n - 1:
            run = dec_in * run + recv1[n].astype(F32)
    recv3[i] = send3[i]
    for k in range(1, inner_n):
        j = lax.rem(i + k, inner_n)
        pltpu.make_async_remote_copy(src_ref=send3.at[j], dst_ref=recv3.at[i], send_sem=s3_sem.at[j],
                                     recv_sem=r3_sem.at[i], device_id=(o, j), device_id_type=MESH).start()

    for g in range(groups):
        for w in range(owners_g):
            n = g * owners_g + w

            @pl.when(n != i)
            def _():
                pltpu.make_async_remote_copy(src_ref=send3.at[n], dst_ref=recv3.at[n], send_sem=s3_sem.at[n],
                                             recv_sem=r3_sem.at[n], device_id=(o, n), device_id_type=MESH).wait_recv()

            got = recv3[n].astype(F32)
            for u in range(sub_o):
                ctm[g, pl.ds(w * sub_o + u, modes, stride=SUB), :] = got[u * modes:(u + 1) * modes]
        d = [mode(dtm, g, m) for m in range(modes)]
        init = tuple(mode(atm, g, m) * (mode(ctm, g, m) + mode(zfin, g, m)) for m in range(modes))

        def apply(t2, carry):
            s = list(carry)
            for u in range(2):
                s = [d[m] * s[m] for m in range(modes)]
                where = pl.ds(pl.multiple_of((t2 * 2 + u) * SUB, SUB), SUB)
                base[g, where, :] = qtm[g, where, :] * (base[g, where, :] + tree(s))
            return tuple(s)

        lax.fori_loop(0, rows // 2, apply, init)

        def settle(c, _):
            for s in range(SUB):
                v = base[g, pl.ds(c * (CHUNK * SUB) + s, CHUNK, stride=SUB), :].astype(BF16)
                outb[pl.ds(pl.multiple_of(c * CHUNK, CHUNK), CHUNK), pl.ds(g * GROUP + s * LANE, LANE)] = v
            return 0

        lax.fori_loop(0, chunks, settle, 0)
        cols = pl.ds(g * GROUP, GROUP)
        pltpu.make_async_copy(outb.at[:, cols], out.at[:, cols], out_sem.at[g]).start()

    halo.wait_send()
    for n in range(inner_n):
        @pl.when(n != i)
        def _():
            for src, sem in ((send1, s1_sem), (send3, s3_sem)):
                pltpu.make_async_remote_copy(src_ref=src.at[n], dst_ref=src.at[n], send_sem=sem.at[n],
                                             recv_sem=sem.at[n], device_id=(o, n), device_id_type=MESH).wait_send()
    for k in range(1, outer_n):
        @pl.when(o + k < outer_n)
        def _():
            pltpu.make_async_remote_copy(src_ref=send2, dst_ref=send2, send_sem=s2_sem.at[k], recv_sem=s2_sem.at[k],
                                         device_id=(o, i), device_id_type=MESH).wait_send()
    for g in range(groups):
        cols = pl.ds(g * GROUP, GROUP)
        pltpu.make_async_copy(outb.at[:, cols], out.at[:, cols], out_sem.at[g]).wait()


def solution(mesh):
    outer_n, inner_n = mesh.shape["outer"], mesh.shape["inner"]

    def on_device(projected, short_taps, rates, residues, skip_gain):
        rows, width = projected.shape
        channels, modes = rates.shape
        groups = channels // GROUP
        per_owner = channels // inner_n
        block = modes * per_owner // LANE
        any_spec = pl.BlockSpec(memory_space=pl.ANY)
        dma = pltpu.SemaphoreType.DMA
        tm = pltpu.VMEM((groups, rows * SUB, LANE), F32)
        pm = pltpu.VMEM((groups, modes * SUB, LANE), F32)
        return pl.pallas_call(
            functools.partial(kernel, (outer_n, inner_n, rows, channels, modes)),
            out_shape=jax.ShapeDtypeStruct((rows, channels), BF16),
            in_specs=[any_spec] * 5,
            out_specs=any_spec,
            scratch_shapes=[
                pltpu.VMEM((rows, width), BF16), tm, tm, tm, tm,
                pltpu.VMEM((3, width), F32), pltpu.VMEM((modes, channels), F32), pltpu.VMEM((modes, channels), F32),
                pltpu.VMEM((groups * SUB, LANE), F32), pltpu.VMEM((3 * 3 * groups * SUB, LANE), F32),
                pm, pm, pm, pm,
                pltpu.VMEM((groups, 2 * SUB, LANE), F32), pm, pm,
                pltpu.VMEM((3 * groups, 2 * SUB, LANE), BF16), pltpu.VMEM((3 * groups, 2 * SUB, LANE), BF16),
                pltpu.VMEM((inner_n, block, LANE), BF16), pltpu.VMEM((inner_n, block, LANE), BF16),
                pltpu.VMEM((block, LANE), BF16), pltpu.VMEM((outer_n, block, LANE), BF16),
                pltpu.VMEM((inner_n, block, LANE), BF16), pltpu.VMEM((inner_n, block, LANE), BF16),
                pltpu.VMEM((rows, channels), BF16),
                dma((3 * groups + 1,)), dma((4,)), dma((groups,)), dma, dma,
                dma((inner_n,)), dma((inner_n,)), dma((outer_n,)), dma((outer_n,)), dma((inner_n,)), dma((inner_n,)),
            ],
            compiler_params=pltpu.CompilerParams(collective_id=0, has_side_effects=True,
                                                 vmem_limit_bytes=48 * 1024 * 1024),
            name="modal_scan",
        )(projected, short_taps, rates.T, residues.T, skip_gain.reshape(groups * SUB, LANE))

    return jax.shard_map(
        on_device, mesh=mesh,
        in_specs=(P(("outer", "inner"), None), P(), P(), P(), P()),
        out_specs=P(("outer", "inner"), None), check_vma=False,
    )
```

```python
import functools

import jax
import jax.numpy as jnp
from jax import lax
from jax.experimental import pallas as pl
from jax.experimental.pallas import tpu as pltpu
from jax.sharding import PartitionSpec as P

MESH = pl.DeviceIdType.MESH
F32 = jnp.float32
BF16 = jnp.bfloat16
SUB = 8
LANE = 128
GROUP = SUB * LANE
CHUNK = 16


def kernel(dims, proj, taps_in, rates_in, resid_in, skip_in, out, raw, ktm, vtm, qtm, base, taps_n, rate_n, res_n,
           skip_v, taps_t, rtm, dtm, atm, zfin, edge, stg, ctm, hsend, hrecv, send1, recv1, send2, recv2, send3, recv3,
           outb, in_sem, par_sem, out_sem, hs_sem, hr_sem, s1_sem, r1_sem, s2_sem, r2_sem, s3_sem, r3_sem):
    outer_n, inner_n, rows, channels, modes = dims
    groups = channels // GROUP
    chunks = rows // CHUNK
    per_owner = channels // inner_n
    owners_g = GROUP // per_owner
    block = modes * per_owner // LANE
    sub_o = per_owner // LANE
    last = rows - CHUNK
    o = lax.axis_index("outer")
    i = lax.axis_index("inner")
    p = o * inner_n + i
    total = outer_n * inner_n
    nxt, prv = lax.rem(p + 1, total), lax.rem(p + total - 1, total)
    nxt_id = (nxt // inner_n, lax.rem(nxt, inner_n))
    prv_id = (prv // inner_n, lax.rem(prv, inner_n))

    bar = pltpu.get_barrier_semaphore()
    for k in range(1, inner_n):
        pl.semaphore_signal(bar, inc=1, device_id=(o, lax.rem(i + k, inner_n)), device_id_type=MESH)
    for k in range(1, outer_n):
        pl.semaphore_signal(bar, inc=1, device_id=(lax.rem(o + k, outer_n), i), device_id_type=MESH)
    pl.semaphore_signal(bar, inc=1, device_id=nxt_id, device_id_type=MESH)
    pl.semaphore_signal(bar, inc=1, device_id=prv_id, device_id_type=MESH)

    tail_cp = pltpu.make_async_copy(proj.at[pl.ds(last, CHUNK), :], raw.at[pl.ds(last, CHUNK), :], in_sem.at[3 * groups])
    tail_cp.start()
    par_cps = [pltpu.make_async_copy(a, b, par_sem.at[n]) for n, (a, b) in enumerate(
        ((taps_in, taps_n), (rates_in, rate_n), (resid_in, res_n), (skip_in, skip_v)))]
    for cp in par_cps:
        cp.start()

    def in_copy(f, g):
        cols = pl.ds((f * groups + g) * GROUP, GROUP)
        return pltpu.make_async_copy(proj.at[pl.ds(0, last), cols], raw.at[pl.ds(0, last), cols],
                                     in_sem.at[f * groups + g])

    for g in range(groups):
        in_copy(1, g).start()
        in_copy(2, g).start()
    for g in range(groups):
        in_copy(0, g).start()
    tms = (qtm, ktm, vtm)

    def relay_chunk(f, g, c):
        for s in range(SUB):
            col = (f * groups + g) * GROUP + s * LANE
            v = raw[pl.ds(pl.multiple_of(c * CHUNK, CHUNK), CHUNK), pl.ds(col, LANE)].astype(F32)
            tms[f][g, pl.ds(c * (CHUNK * SUB) + s, CHUNK, stride=SUB), :] = v

    tail_cp.wait()
    for f in range(3):
        for g in range(groups):
            relay_chunk(f, g, chunks - 1)
            hsend[f * groups + g] = tms[f][g, pl.ds((rows - 2) * SUB, 2 * SUB), :].astype(BF16)

    for cp in par_cps:
        cp.wait()
    for fg in range(3 * groups):
        for s in range(SUB):
            taps_t[pl.ds(fg * 3 * SUB + s, 3, stride=SUB), :] = taps_n[:, pl.ds(fg * GROUP + s * LANE, LANE)]
    for g in range(groups):
        for s in range(SUB):
            cols = pl.ds(g * GROUP + s * LANE, LANE)
            r = rate_n[:, cols]
            rtm[g, pl.ds(s, modes, stride=SUB), :] = r
            dtm[g, pl.ds(s, modes, stride=SUB), :] = jnp.exp(-r)
            atm[g, pl.ds(s, modes, stride=SUB), :] = res_n[:, cols] * jnp.sqrt(2.0 * r)

    def tap(f, g):
        return [taps_t[pl.ds(((f * groups + g) * 3 + j) * SUB, SUB), :] for j in range(3)]

    def mode(ref, g, m):
        return ref[g, pl.ds(m * SUB, SUB), :]

    def tok(ref, g, t):
        return ref[g, pl.ds(pl.multiple_of(t * SUB, SUB), SUB), :]

    def tree(vals):
        vals = list(vals)
        while len(vals) > 1:
            vals = [a + b for a, b in zip(vals[::2], vals[1::2])] + (vals[-1:] if len(vals) % 2 else [])
        return vals[0]

    def recur(g):
        d = [mode(dtm, g, m) for m in range(modes)]
        tk, tv = tap(1, g), tap(2, g)
        sk = skip_v[pl.ds(g * SUB, SUB), :]

        def body(t2, carry):
            z = list(carry[:modes])
            k1, k2, v1, v2 = carry[modes:]
            xs = []
            for u in range(2):
                k0, v0 = tok(ktm, g, t2 * 2 + u), tok(vtm, g, t2 * 2 + u)
                xs.append((tk[0] * k0 + tk[1] * k1 + tk[2] * k2) * (tv[0] * v0 + tv[1] * v1 + tv[2] * v2))
                k1, k2, v1, v2 = k0, k1, v0, v1
            accs = [[xs[0] * sk, None, None, None], [xs[1] * sk, None, None, None]]
            for m in range(modes):
                a = mode(atm, g, m)
                for u in range(2):
                    z[m] = d[m] * z[m] + xs[u]
                    term = a * z[m]
                    old = accs[u][m % 4]
                    accs[u][m % 4] = term if old is None else old + term
            for u in range(2):
                base[g, pl.ds(pl.multiple_of((t2 * 2 + u) * SUB, SUB), SUB), :] = tree(accs[u])
            return (*z, k1, k2, v1, v2)

        zero = jnp.zeros((SUB, LANE), F32)
        init = (*([zero] * modes), tok(ktm, g, 1), tok(ktm, g, 0), tok(vtm, g, 1), tok(vtm, g, 0))
        done = lax.fori_loop(1, rows // 2, body, init)
        for m in range(modes):
            zfin[g, pl.ds(m * SUB, SUB), :] = done[m]

    halo = pltpu.make_async_remote_copy(src_ref=hsend, dst_ref=hrecv, send_sem=hs_sem, recv_sem=hr_sem,
                                        device_id=nxt_id, device_id_type=MESH)
    for g in range(groups):
        if g == groups // 2:
            pl.semaphore_wait(bar, inner_n + outer_n)
            halo.start()
        for f in (1, 2):
            in_copy(f, g).wait()

        def relay(c, _):
            relay_chunk(1, g, c)
            relay_chunk(2, g, c)
            return 0

        lax.fori_loop(0, chunks - 1, relay, 0)
        recur(g)

    halo.wait_recv()
    first = p == 0

    def halo_of(f, g):
        both = hrecv[f * groups + g].astype(F32)
        both = jnp.where(first, jnp.zeros_like(both), both)
        return both[:SUB], both[SUB:]

    for g in range(groups):
        feats = []
        for f in (1, 2):
            h2, h1 = halo_of(f, g)
            t0, t1, t2 = tap(f, g)
            e0, e1 = tok(tms[f], g, 0), tok(tms[f], g, 1)
            feats.append((t0 * e0 + t1 * h1 + t2 * h2, t0 * e1 + t1 * e0 + t2 * h1))
        x0, x1 = feats[0][0] * feats[1][0], feats[0][1] * feats[1][1]
        edge[g, pl.ds(0, SUB), :] = x0
        edge[g, pl.ds(SUB, SUB), :] = x1
        for m in range(modes):
            state = mode(zfin, g, m) + jnp.exp(-(rows - 2.0) * mode(rtm, g, m)) * (mode(dtm, g, m) * x0 + x1)
            stg[g, pl.ds(m, SUB, stride=modes), :] = state
        for w in range(owners_g):
            j = g * owners_g + w
            val = stg[g, pl.ds(w * block, block), :].astype(BF16)

            @pl.when(j == i)
            def _():
                recv1[j] = val

            @pl.when(j != i)
            def _():
                send1[j] = val
                pltpu.make_async_remote_copy(src_ref=send1.at[j], dst_ref=recv1.at[i], send_sem=s1_sem.at[j],
                                             recv_sem=r1_sem.at[i], device_id=(o, j), device_id_type=MESH).start()

    for g in range(groups):
        in_copy(0, g).wait()

        def relay_q(c, _):
            relay_chunk(0, g, c)
            return 0

        lax.fori_loop(0, chunks - 1, relay_q, 0)
        t0, t1, t2 = tap(0, g)
        h2, h1 = halo_of(0, g)

        def gate(t, carry):
            q1, q2 = carry
            for u in range(2):
                q0 = tok(qtm, g, t * 2 + u)
                qtm[g, pl.ds(pl.multiple_of((t * 2 + u) * SUB, SUB), SUB), :] = t0 * q0 + t1 * q1 + t2 * q2
                q1, q2 = q0, q1
            return q1, q2

        lax.fori_loop(0, rows // 2, gate, (h1, h2))

    for n in range(inner_n):
        @pl.when(n != i)
        def _():
            pltpu.make_async_remote_copy(src_ref=send1.at[n], dst_ref=recv1.at[n], send_sem=s1_sem.at[n],
                                         recv_sem=r1_sem.at[n], device_id=(o, n), device_id_type=MESH).wait_recv()

    def own_rate(w):
        return rate_n[:, pl.ds(pl.multiple_of(i * per_owner + w * LANE, LANE), LANE)]

    own = jnp.concatenate([own_rate(w) for w in range(sub_o)], axis=0)
    dec_in = jnp.exp(-float(rows) * own)
    dec_out = jnp.exp(-float(rows * inner_n) * own)
    run = recv1[0].astype(F32)
    for n in range(1, inner_n):
        run = dec_in * run + recv1[n].astype(F32)
    send2[...] = run.astype(BF16)
    for k in range(1, outer_n):
        @pl.when(o + k < outer_n)
        def _():
            pltpu.make_async_remote_copy(src_ref=send2, dst_ref=recv2.at[o], send_sem=s2_sem.at[k],
                                         recv_sem=r2_sem.at[o], device_id=(o + k, i), device_id_type=MESH).start()

    for g in range(groups):
        x0, x1 = edge[g, pl.ds(0, SUB), :], edge[g, pl.ds(SUB, SUB), :]
        sk = skip_v[pl.ds(g * SUB, SUB), :]
        lead = tree([mode(atm, g, m) * jnp.exp(mode(rtm, g, m)) for m in range(modes)])
        base[g, pl.ds(0, SUB), :] = sk * x0 - x1 * lead
        base[g, pl.ds(SUB, SUB), :] = sk * x1
        for m in range(modes):
            r = mode(rtm, g, m)
            zfin[g, pl.ds(m * SUB, SUB), :] = jnp.exp(r) * x0 + jnp.exp(2.0 * r) * x1

    def add_outer(n, acc):
        pltpu.make_async_remote_copy(src_ref=send2, dst_ref=recv2.at[n], send_sem=s2_sem.at[0],
                                     recv_sem=r2_sem.at[n], device_id=(n, i), device_id_type=MESH).wait_recv()
        return dec_out * acc + recv2[n].astype(F32)

    run = lax.fori_loop(0, o, add_outer, jnp.zeros((block, LANE), F32))
    for n in range(inner_n):
        send3[n] = run.astype(BF16)
        if n < inner_n - 1:
            run = dec_in * run + recv1[n].astype(F32)
    recv3[i] = send3[i]
    for k in range(1, inner_n):
        j = lax.rem(i + k, inner_n)
        pltpu.make_async_remote_copy(src_ref=send3.at[j], dst_ref=recv3.at[i], send_sem=s3_sem.at[j],
                                     recv_sem=r3_sem.at[i], device_id=(o, j), device_id_type=MESH).start()

    for g in range(groups):
        for w in range(owners_g):
            n = g * owners_g + w

            @pl.when(n != i)
            def _():
                pltpu.make_async_remote_copy(src_ref=send3.at[n], dst_ref=recv3.at[n], send_sem=s3_sem.at[n],
                                             recv_sem=r3_sem.at[n], device_id=(o, n), device_id_type=MESH).wait_recv()

            got = recv3[n].astype(F32)
            for u in range(sub_o):
                ctm[g, pl.ds(w * sub_o + u, modes, stride=SUB), :] = got[u * modes:(u + 1) * modes]
        d = [mode(dtm, g, m) for m in range(modes)]
        init = tuple(mode(atm, g, m) * (mode(ctm, g, m) + mode(zfin, g, m)) for m in range(modes))

        def apply(t2, carry):
            s = list(carry)
            for u in range(2):
                s = [d[m] * s[m] for m in range(modes)]
                where = pl.ds(pl.multiple_of((t2 * 2 + u) * SUB, SUB), SUB)
                base[g, where, :] = qtm[g, where, :] * (base[g, where, :] + tree(s))
            return tuple(s)

        lax.fori_loop(0, rows // 2, apply, init)

        def settle(c, _):
            for s in range(SUB):
                v = base[g, pl.ds(c * (CHUNK * SUB) + s, CHUNK, stride=SUB), :].astype(BF16)
                outb[pl.ds(pl.multiple_of(c * CHUNK, CHUNK), CHUNK), pl.ds(g * GROUP + s * LANE, LANE)] = v
            return 0

        lax.fori_loop(0, chunks, settle, 0)
        cols = pl.ds(g * GROUP, GROUP)
        pltpu.make_async_copy(outb.at[:, cols], out.at[:, cols], out_sem.at[g]).start()

    halo.wait_send()
    for n in range(inner_n):
        @pl.when(n != i)
        def _():
            for src, sem in ((send1, s1_sem), (send3, s3_sem)):
                pltpu.make_async_remote_copy(src_ref=src.at[n], dst_ref=src.at[n], send_sem=sem.at[n],
                                             recv_sem=sem.at[n], device_id=(o, n), device_id_type=MESH).wait_send()
    for k in range(1, outer_n):
        @pl.when(o + k < outer_n)
        def _():
            pltpu.make_async_remote_copy(src_ref=send2, dst_ref=send2, send_sem=s2_sem.at[k], recv_sem=s2_sem.at[k],
                                         device_id=(o, i), device_id_type=MESH).wait_send()
    for g in range(groups):
        cols = pl.ds(g * GROUP, GROUP)
        pltpu.make_async_copy(outb.at[:, cols], out.at[:, cols], out_sem.at[g]).wait()


def solution(mesh):
    outer_n, inner_n = mesh.shape["outer"], mesh.shape["inner"]

    def on_device(projected, short_taps, rates, residues, skip_gain):
        rows, width = projected.shape
        channels, modes = rates.shape
        groups = channels // GROUP
        per_owner = channels // inner_n
        block = modes * per_owner // LANE
        any_spec = pl.BlockSpec(memory_space=pl.ANY)
        dma = pltpu.SemaphoreType.DMA
        tm = pltpu.VMEM((groups, rows * SUB, LANE), F32)
        pm = pltpu.VMEM((groups, modes * SUB, LANE), F32)
        return pl.pallas_call(
            functools.partial(kernel, (outer_n, inner_n, rows, channels, modes)),
            out_shape=jax.ShapeDtypeStruct((rows, channels), BF16),
            in_specs=[any_spec] * 5,
            out_specs=any_spec,
            scratch_shapes=[
                pltpu.VMEM((rows, width), BF16), tm, tm, tm, tm,
                pltpu.VMEM((3, width), F32), pltpu.VMEM((modes, channels), F32), pltpu.VMEM((modes, channels), F32),
                pltpu.VMEM((groups * SUB, LANE), F32), pltpu.VMEM((3 * 3 * groups * SUB, LANE), F32),
                pm, pm, pm, pm,
                pltpu.VMEM((groups, 2 * SUB, LANE), F32), pm, pm,
                pltpu.VMEM((3 * groups, 2 * SUB, LANE), BF16), pltpu.VMEM((3 * groups, 2 * SUB, LANE), BF16),
                pltpu.VMEM((inner_n, block, LANE), BF16), pltpu.VMEM((inner_n, block, LANE), BF16),
                pltpu.VMEM((block, LANE), BF16), pltpu.VMEM((outer_n, block, LANE), BF16),
                pltpu.VMEM((inner_n, block, LANE), BF16), pltpu.VMEM((inner_n, block, LANE), BF16),
                pltpu.VMEM((rows, channels), BF16),
                dma((3 * groups + 1,)), dma((4,)), dma((groups,)), dma, dma,
                dma((inner_n,)), dma((inner_n,)), dma((outer_n,)), dma((outer_n,)), dma((inner_n,)), dma((inner_n,)),
            ],
            compiler_params=pltpu.CompilerParams(collective_id=0, has_side_effects=True,
                                                 vmem_limit_bytes=60 * 1024 * 1024),
            name="modal_scan",
        )(projected, short_taps, rates.T, residues.T, skip_gain.reshape(groups * SUB, LANE))

    return jax.shard_map(
        on_device, mesh=mesh,
        in_specs=(P(("outer", "inner"), None), P(), P(), P(), P()),
        out_specs=P(("outer", "inner"), None), check_vma=False,
    )
```

```python
import functools

import jax
import jax.numpy as jnp
from jax import lax
from jax.experimental import pallas as pl
from jax.experimental.pallas import tpu as pltpu
from jax.sharding import PartitionSpec as P

MESH = pl.DeviceIdType.MESH
F32 = jnp.float32
BF16 = jnp.bfloat16
SUB = 8
LANE = 128
GROUP = SUB * LANE
CHUNK = 16
RING = 8


def kernel(dims, proj, taps_in, rates_in, resid_in, skip_in, out, raw, ktmp, vtmp, ktmp2, vtmp2, ttmp, qtm, xs, base, taps_n,
           rate_n, res_n, skip_v, taps_t, rtm, dtm, d16, atm, ztm, ends, edge, head, stg, ctm, pre, powr, hsend, hrecv,
           send1, recv1, send2, recv2, send3, recv3, ytmp, ytmp2, outb, in_sem, par_sem, out_sem, hs_sem, hr_sem, s1_sem,
           r1_sem, s2_sem, r2_sem, s3_sem, r3_sem):
    outer_n, inner_n, rows, channels, modes = dims
    groups = channels // GROUP
    chunks = rows // CHUNK
    n1 = channels // LANE
    total = outer_n * inner_n
    n2 = total // n1
    last = rows - CHUNK
    p = lax.axis_index("outer") * inner_n + lax.axis_index("inner")
    e = lax.rem(p, n1)
    h = p // n1
    far = lax.rem(p, RING) == RING - 1
    near = lax.rem(p, RING) != 0

    def dev(r):
        return (r // inner_n, lax.rem(r, inner_n))

    def mate(n):
        return dev(h * n1 + n)

    def ring_order():
        for dz in (4, 3, 5, 2, 6, 1, 7, 0):
            for hi in range(n1 // RING):
                if dz or hi:
                    yield lax.rem(e // RING + hi, n1 // RING) * RING + lax.rem(lax.rem(e, RING) + dz, RING)

    def remote(src, dst, ssem, rsem, to):
        return pltpu.make_async_remote_copy(src_ref=src, dst_ref=dst, send_sem=ssem, recv_sem=rsem, device_id=to,
                                            device_id_type=MESH)

    kv = pl.ds(channels, 2 * channels)
    tails = [pltpu.make_async_copy(proj.at[pl.ds(last, CHUNK), c], raw.at[pl.ds(last, CHUNK), c], in_sem.at[3 * groups + n])
             for n, c in enumerate((kv, pl.ds(0, channels)))]
    tails[0].start()
    par_cps = [pltpu.make_async_copy(a, b, par_sem.at[n]) for n, (a, b) in enumerate(
        ((rates_in, rate_n), (taps_in, taps_n), (resid_in, res_n), (skip_in, skip_v)))]
    par_cps[0].start()
    par_cps[1].start()

    def in_copy(f, g):
        cols = pl.ds((f * groups + g) * GROUP, GROUP)
        return pltpu.make_async_copy(proj.at[pl.ds(0, last), cols], raw.at[pl.ds(0, last), cols],
                                     in_sem.at[f * groups + g])

    for g in range(groups):
        in_copy(1, g).start()
        in_copy(2, g).start()
    par_cps[2].start()
    par_cps[3].start()
    tails[1].start()
    for g in range(groups):
        in_copy(0, g).start()

    bar = pltpu.get_barrier_semaphore()
    nxt, prv = dev(lax.rem(p + 1, total)), dev(lax.rem(p + total - 1, total))
    for to in (nxt, prv):
        pl.semaphore_signal(bar, inc=1, device_id=to, device_id_type=MESH)
    for k in range(1, n2):
        pl.semaphore_signal(bar, inc=1, device_id=dev(lax.rem(h + k, n2) * n1 + e), device_id_type=MESH)
    for n in ring_order():
        pl.semaphore_signal(bar, inc=1, device_id=mate(n), device_id_type=MESH)

    def relay(dst, row, f, g, c):
        for s in range(SUB):
            col = (f * groups + g) * GROUP + s * LANE
            v = raw[pl.ds(pl.multiple_of(c * CHUNK, CHUNK), CHUNK), pl.ds(col, LANE)].astype(F32)
            dst[pl.ds(row + s, CHUNK, stride=SUB), :] = v

    def tail_of(f):
        for g in range(groups):
            relay(ttmp.at[f * groups + g], 0, f, g, chunks - 1)
            hsend[f * groups + g] = ttmp[f * groups + g, pl.ds((CHUNK - 2) * SUB, 2 * SUB), :].astype(BF16)

    tails[0].wait()
    tail_of(1)
    tail_of(2)
    kv_blocks, q_blocks = pl.ds(groups, 2 * groups), pl.ds(0, groups)
    halo = remote(hsend.at[kv_blocks], hrecv.at[kv_blocks], hs_sem.at[0], hr_sem.at[0], nxt)
    halo_q = remote(hsend.at[q_blocks], hrecv.at[q_blocks], hs_sem.at[1], hr_sem.at[1], nxt)

    def send_halo():
        pl.semaphore_wait(bar, n1 + n2)
        halo.start()

    pl.when(far)(send_halo)

    par_cps[0].wait()
    par_cps[1].wait()
    for f in (1, 2):
        for g in range(groups):
            fg = f * groups + g
            for s in range(SUB):
                taps_t[pl.ds(fg * 3 * SUB + s, 3, stride=SUB), :] = taps_n[:, pl.ds(fg * GROUP + s * LANE, LANE)]
    for g in range(groups):
        for s in range(SUB):
            rtm[g, pl.ds(s, modes, stride=SUB), :] = rate_n[:, pl.ds(g * GROUP + s * LANE, LANE)]
        r = rtm[g]
        dtm[g] = jnp.exp(-r)
        d16[g] = jnp.exp(-float(CHUNK) * r)

    def tap(f, g):
        return [taps_t[pl.ds(((f * groups + g) * 3 + j) * SUB, SUB), :] for j in range(3)]

    def mode(ref, g, m):
        return ref[g, pl.ds(m * SUB, SUB), :]

    def at(t):
        return pl.ds(pl.multiple_of(t * SUB, SUB), SUB)

    def tree(vals):
        vals = list(vals)
        while len(vals) > 1:
            vals = [a + b for a, b in zip(vals[::2], vals[1::2])] + (vals[-1:] if len(vals) % 2 else [])
        return vals[0]

    zero = jnp.zeros((SUB, LANE), F32)

    def states(g):
        d = [mode(dtm, g, m) for m in range(modes)]
        tk, tv = tap(1, g), tap(2, g)
        relay(ktmp, 0, 1, g, 0)
        relay(vtmp, 0, 2, g, 0)
        head[g, pl.ds(0, 2 * SUB), :] = ktmp[pl.ds(0, 2 * SUB), :]
        head[g, pl.ds(2 * SUB, 2 * SUB), :] = vtmp[pl.ds(0, 2 * SUB), :]
        for m in range(modes):
            ztm[g, pl.ds(m * SUB, SUB), :] = zero

        def chunk(c, bufs, spare, carry):
            ahead = jnp.minimum(c + 1, chunks - 1)
            relay(spare[0], 0, 1, g, ahead)
            relay(spare[1], 0, 2, g, ahead)
            k1, k2, v1, v2 = carry
            u = [None] * modes
            for t in range(CHUNK):
                k0, v0 = bufs[0][pl.ds(t * SUB, SUB), :], bufs[1][pl.ds(t * SUB, SUB), :]
                x = (tk[0] * k0 + tk[1] * k1 + tk[2] * k2) * (tv[0] * v0 + tv[1] * v1 + tv[2] * v2)
                if t < 2:
                    x = jnp.where(c == 0, zero, x)
                k1, k2, v1, v2 = k0, k1, v0, v1
                xs[g, at(c * CHUNK + t), :] = x
                u = [x if u[m] is None else d[m] * u[m] + x for m in range(modes)]
            for m in range(modes):
                ends[g, at(c * modes + m), :] = u[m]
                ztm[g, pl.ds(m * SUB, SUB), :] = mode(d16, g, m) * mode(ztm, g, m) + u[m]
            return k1, k2, v1, v2

        def pair(j, carry):
            carry = chunk(2 * j, (ktmp, vtmp), (ktmp2, vtmp2), carry)
            return chunk(2 * j + 1, (ktmp2, vtmp2), (ktmp, vtmp), carry)

        lax.fori_loop(0, chunks // 2, pair, (zero, zero, zero, zero))

    first = p == 0

    def halo_of(f, g):
        both = hrecv[f * groups + g].astype(F32)
        both = jnp.where(first, jnp.zeros_like(both), both)
        return both[:SUB], both[SUB:]

    def emit(g):
        feats = []
        for n, f in enumerate((1, 2)):
            h2, h1 = halo_of(f, g)
            t0, t1, t2 = tap(f, g)
            e0, e1 = head[g, pl.ds(2 * n * SUB, SUB), :], head[g, pl.ds((2 * n + 1) * SUB, SUB), :]
            feats.append((t0 * e0 + t1 * h1 + t2 * h2, t0 * e1 + t1 * e0 + t2 * h1))
        x0, x1 = feats[0][0] * feats[1][0], feats[0][1] * feats[1][1]
        edge[g, pl.ds(0, SUB), :] = x0
        edge[g, pl.ds(SUB, SUB), :] = x1
        for m in range(modes):
            state = mode(ztm, g, m) + jnp.exp(-(rows - 2.0) * mode(rtm, g, m)) * (mode(dtm, g, m) * x0 + x1)
            stg[pl.ds(g * SUB * modes + m, SUB, stride=modes), :] = state
        for s in range(SUB):
            n = g * SUB + s
            send1[n] = stg[pl.ds(n * modes, modes), :].astype(BF16)
        for s in range(SUB):
            n = g * SUB + s

            @pl.when(n == e)
            def _():
                recv1[n] = send1[n]

            @pl.when(n != e)
            def _():
                remote(send1.at[n], recv1.at[e], s1_sem.at[n], r1_sem.at[e], mate(n)).start()

    early = groups - 1
    for g in range(groups):
        for f in (1, 2):
            in_copy(f, g).wait()
        states(g)
        if g == (groups - 1) // 2:
            pl.when(jnp.logical_not(far))(send_halo)
        if g == early - 1:
            @pl.when(near)
            def _():
                halo.wait_recv()
                for n in range(early):
                    emit(n)

    def rest():
        halo.wait_recv()
        for n in range(early):
            emit(n)

    if early:
        pl.when(jnp.logical_not(near))(rest)
    else:
        halo.wait_recv()
    emit(groups - 1)

    tails[1].wait()
    tail_of(0)
    halo_q.start()
    par_cps[2].wait()
    par_cps[3].wait()
    for g in range(groups):
        for s in range(SUB):
            taps_t[pl.ds(g * 3 * SUB + s, 3, stride=SUB), :] = taps_n[:, pl.ds(g * GROUP + s * LANE, LANE)]
            cols = pl.ds(g * GROUP + s * LANE, LANE)
            atm[g, pl.ds(s, modes, stride=SUB), :] = res_n[:, cols] * jnp.sqrt(2.0 * rate_n[:, cols])
    for g in range(groups):
        in_copy(0, g).wait()
        t0, t1, t2 = tap(0, g)

        def gate(c, bufs, spare, carry):
            relay(spare, 0, 0, g, jnp.minimum(c + 1, chunks - 1))
            q1, q2 = carry
            for t in range(CHUNK):
                q0 = bufs[pl.ds(t * SUB, SUB), :]
                qtm[g, at(c * CHUNK + t), :] = t0 * q0 + t1 * q1 + t2 * q2
                q1, q2 = q0, q1
            return q1, q2

        def gates(j, carry):
            return gate(2 * j + 1, ktmp2, ktmp, gate(2 * j, ktmp, ktmp2, carry))

        relay(ktmp, 0, 0, g, 0)
        lax.fori_loop(0, chunks // 2, gates, (zero, zero))

    own = rate_n[:, pl.ds(pl.multiple_of(e * LANE, LANE), LANE)]
    dec_in = jnp.exp(-float(rows) * own)
    dec_out = jnp.exp(-float(rows * n1) * own)
    run = jnp.zeros((modes, LANE), F32)
    for n in range(n1):
        pre[n] = run

        @pl.when(n != e)
        def _():
            remote(send1.at[n], recv1.at[n], s1_sem.at[n], r1_sem.at[n], mate(n)).wait_recv()

        run = dec_in * run + recv1[n].astype(F32)
    send2[...] = run.astype(BF16)
    for k in range(n2 - 1, 0, -1):
        @pl.when(h + k < n2)
        def _():
            remote(send2, recv2.at[h], s2_sem.at[k], r2_sem.at[h], dev((h + k) * n1 + e)).start()

    power = jnp.ones((modes, LANE), F32)
    for n in range(n1):
        powr[n] = power
        power = power * dec_in

    def local(g):
        d = [mode(dtm, g, m) for m in range(modes)]
        a = [mode(atm, g, m) for m in range(modes)]
        taps = []
        for j in range(CHUNK):
            taps.append(tree(a))
            a = [d[m] * a[m] for m in range(modes)]
        taps[0] = taps[0] + skip_v[pl.ds(g * SUB, SUB), :]

        def body(c, _):
            x = [xs[g, at(c * CHUNK + t), :] for t in range(CHUNK)]
            for t in range(CHUNK):
                base[g, at(c * CHUNK + t), :] = tree([taps[j] * x[t - j] for j in range(t + 1)])
            for m in range(modes):
                ends[g, at(c * modes + m), :] = mode(atm, g, m) * ends[g, at(c * modes + m), :]
            return 0

        lax.fori_loop(0, chunks, body, 0)

    def fix_edge(g):
        x0, x1 = edge[g, pl.ds(0, SUB), :], edge[g, pl.ds(SUB, SUB), :]
        sk = skip_v[pl.ds(g * SUB, SUB), :]
        lead = tree([mode(atm, g, m) * jnp.exp(mode(rtm, g, m)) for m in range(modes)])
        base[g, pl.ds(0, SUB), :] = sk * x0 - x1 * lead
        base[g, pl.ds(SUB, SUB), :] = sk * x1
        for m in range(modes):
            r = mode(rtm, g, m)
            ztm[g, pl.ds(m * SUB, SUB), :] = jnp.exp(r) * x0 + jnp.exp(2.0 * r) * x1

    split = (groups + 1) // 2
    for g in range(split):
        local(g)

    def add_outer(n, acc):
        remote(send2, recv2.at[n], s2_sem.at[0], r2_sem.at[n], dev(n * n1 + e)).wait_recv()
        return dec_out * acc + recv2[n].astype(F32)

    carried = lax.fori_loop(0, h, add_outer, jnp.zeros((modes, LANE), F32))
    for n in range(n1):
        send3[n] = (pre[n] + powr[n] * carried).astype(BF16)
    recv3[e] = send3[e]
    for n in ring_order():
        remote(send3.at[n], recv3.at[e], s3_sem.at[n], r3_sem.at[e], mate(n)).start()
    for g in range(split, groups):
        local(g)
    for g in range(groups):
        fix_edge(g)
    halo_q.wait_recv()
    for g in range(groups):
        h2, h1 = halo_of(0, g)
        t0, t1, t2 = tap(0, g)
        qtm[g, pl.ds(0, SUB), :] = qtm[g, pl.ds(0, SUB), :] + (t1 * h1 + t2 * h2)
        qtm[g, pl.ds(SUB, SUB), :] = qtm[g, pl.ds(SUB, SUB), :] + t2 * h1

    for g in range(groups):
        for s in range(SUB):
            n = g * SUB + s

            @pl.when(n != e)
            def _():
                remote(send3.at[n], recv3.at[n], s3_sem.at[n], r3_sem.at[n], mate(n)).wait_recv()

            ctm[g, pl.ds(s, modes, stride=SUB), :] = recv3[n].astype(F32)
        d = [mode(dtm, g, m) for m in range(modes)]
        init = tuple(mode(atm, g, m) * (mode(ctm, g, m) + mode(ztm, g, m)) for m in range(modes))

        def apply(c, buf, carry):
            s = list(carry)
            for t in range(CHUNK):
                s = [d[m] * s[m] for m in range(modes)]
                here = at(c * CHUNK + t)
                buf[pl.ds(t * SUB, SUB), :] = qtm[g, here, :] * (base[g, here, :] + tree(s))
            for w in range(SUB):
                v = buf[pl.ds(w, CHUNK, stride=SUB), :].astype(BF16)
                outb[pl.ds(pl.multiple_of(c * CHUNK, CHUNK), CHUNK), pl.ds(g * GROUP + w * LANE, LANE)] = v
            return tuple(s[m] + ends[g, at(c * modes + m), :] for m in range(modes))

        def applies(j, carry):
            return apply(2 * j + 1, ytmp2, apply(2 * j, ytmp, carry))

        lax.fori_loop(0, chunks // 2, applies, init)
        cols = pl.ds(g * GROUP, GROUP)
        pltpu.make_async_copy(outb.at[:, cols], out.at[:, cols], out_sem.at[g]).start()

    halo.wait_send()
    halo_q.wait_send()
    for n in range(n1):
        @pl.when(n != e)
        def _():
            for src, sem in ((send1, s1_sem), (send3, s3_sem)):
                remote(src.at[n], src.at[n], sem.at[n], sem.at[n], mate(n)).wait_send()
    for k in range(1, n2):
        @pl.when(h + k < n2)
        def _():
            remote(send2, send2, s2_sem.at[k], s2_sem.at[k], nxt).wait_send()
    for g in range(groups):
        cols = pl.ds(g * GROUP, GROUP)
        pltpu.make_async_copy(outb.at[:, cols], out.at[:, cols], out_sem.at[g]).wait()


def solution(mesh):
    outer_n, inner_n = mesh.shape["outer"], mesh.shape["inner"]

    def on_device(projected, short_taps, rates, residues, skip_gain):
        rows, width = projected.shape
        channels, modes = rates.shape
        groups = channels // GROUP
        n1 = channels // LANE
        n2 = outer_n * inner_n // n1
        any_spec = pl.BlockSpec(memory_space=pl.ANY)
        dma = pltpu.SemaphoreType.DMA
        tm = pltpu.VMEM((groups, rows * SUB, LANE), F32)
        pm = pltpu.VMEM((groups, modes * SUB, LANE), F32)
        tmp = pltpu.VMEM((CHUNK * SUB, LANE), F32)
        msg = pltpu.VMEM((n1, modes, LANE), BF16)
        return pl.pallas_call(
            functools.partial(kernel, (outer_n, inner_n, rows, channels, modes)),
            out_shape=jax.ShapeDtypeStruct((rows, channels), BF16),
            in_specs=[any_spec] * 5,
            out_specs=any_spec,
            scratch_shapes=[
                pltpu.VMEM((rows, width), BF16), tmp, tmp, tmp, tmp,
                pltpu.VMEM((3 * groups, CHUNK * SUB, LANE), F32), tm, tm, tm,
                pltpu.VMEM((3, width), F32), pltpu.VMEM((modes, channels), F32), pltpu.VMEM((modes, channels), F32),
                pltpu.VMEM((groups * SUB, LANE), F32), pltpu.VMEM((3 * 3 * groups * SUB, LANE), F32),
                pm, pm, pm, pm, pm,
                pltpu.VMEM((groups, rows // CHUNK * modes * SUB, LANE), F32),
                pltpu.VMEM((groups, 2 * SUB, LANE), F32), pltpu.VMEM((groups, 4 * SUB, LANE), F32),
                pltpu.VMEM((groups * SUB * modes, LANE), F32), pm,
                pltpu.VMEM((n1, modes, LANE), F32), pltpu.VMEM((n1, modes, LANE), F32),
                pltpu.VMEM((3 * groups, 2 * SUB, LANE), BF16), pltpu.VMEM((3 * groups, 2 * SUB, LANE), BF16),
                msg, msg, pltpu.VMEM((modes, LANE), BF16), pltpu.VMEM((n2, modes, LANE), BF16), msg, msg,
                tmp, tmp, pltpu.VMEM((rows, channels), BF16),
                dma((3 * groups + 2,)), dma((4,)), dma((groups,)), dma((2,)), dma((2,)),
                dma((n1,)), dma((n1,)), dma((n2,)), dma((n2,)), dma((n1,)), dma((n1,)),
            ],
            compiler_params=pltpu.CompilerParams(collective_id=0, has_side_effects=True,
                                                 vmem_limit_bytes=60 * 1024 * 1024),
            name="modal_scan",
        )(projected, short_taps, rates.T, residues.T, skip_gain.reshape(groups * SUB, LANE))

    return jax.shard_map(
        on_device, mesh=mesh,
        in_specs=(P(("outer", "inner"), None), P(), P(), P(), P()),
        out_specs=P(("outer", "inner"), None), check_vma=False,
    )
```

```python
import functools

import jax
import jax.numpy as jnp
from jax import lax
from jax.experimental import pallas as pl
from jax.experimental.pallas import tpu as pltpu
from jax.sharding import PartitionSpec as P

MESH = pl.DeviceIdType.MESH
F32 = jnp.float32
BF16 = jnp.bfloat16
SUB = 8
LANE = 128
GROUP = SUB * LANE
CHUNK = 16
RING = 8


def kernel(dims, proj, taps_in, rates_in, resid_in, skip_in, out, raw, ktmp, vtmp, ktmp2, vtmp2, ttmp, qtm, xs, base, taps_n,
           rate_n, res_n, skip_v, taps_t, rtm, dtm, d16, atm, ztm, ends, edge, head, stg, ctm, pre, powr, hsend, hrecv, xstage, xwork, xwork2, xsend, xrecv,
           send1, recv1, send2, recv2, send3, recv3, ytmp, ytmp2, in_sem, par_sem, hs_sem, hr_sem, xs_sem, xr_sem,
           s1_sem, r1_sem, s2_sem, r2_sem, s3_sem, r3_sem):
    outer_n, inner_n, rows, channels, modes = dims
    groups = channels // GROUP
    chunks = rows // CHUNK
    n1 = channels // LANE
    total = outer_n * inner_n
    n2 = total // n1
    last = rows - CHUNK
    p = lax.axis_index("outer") * inner_n + lax.axis_index("inner")
    e = lax.rem(p, n1)
    h = p // n1
    z = lax.rem(e, RING)
    hi = e // RING
    high = n1 // RING
    zpg = RING // groups
    near = z != 0
    rim = jnp.logical_or(z == 0, z == RING - 1)
    mine = (z // zpg) * SUB + hi * zpg + lax.rem(z, zpg)

    def far_first(idx):
        if groups == 1:
            return 0
        odd = lax.rem(z, 2)
        off = (2, 1 + 2 * odd, 3 - 2 * odd, 0)
        step = off[idx] if isinstance(idx, int) else jnp.where(
            idx == 0, off[0], jnp.where(idx == 1, off[1], jnp.where(idx == 2, off[2], off[3])))
        return lax.rem(z // zpg + step, groups)

    def owner(n):
        s = lax.rem(n, SUB) if not isinstance(n, int) else n % SUB
        return (s // zpg) * RING + zpg * (n // SUB) + (s % zpg if isinstance(s, int) else lax.rem(s, zpg))

    def own_by(g, s):
        return (s // zpg) * RING + zpg * g + s % zpg

    def dev(r):
        return (r // inner_n, lax.rem(r, inner_n))

    def mate(n):
        return dev(h * n1 + n)

    def ring_order():
        for dz in (4, 3, 5, 2, 6, 1, 7, 0):
            for hi in range(n1 // RING):
                if dz or hi:
                    yield lax.rem(e // RING + hi, n1 // RING) * RING + lax.rem(lax.rem(e, RING) + dz, RING)

    def remote(src, dst, ssem, rsem, to):
        return pltpu.make_async_remote_copy(src_ref=src, dst_ref=dst, send_sem=ssem, recv_sem=rsem, device_id=to,
                                            device_id_type=MESH)

    kv = pl.ds(channels, 2 * channels)
    tails = [pltpu.make_async_copy(proj.at[pl.ds(last, CHUNK), c], raw.at[pl.ds(last, CHUNK), c], in_sem.at[3 * groups + n])
             for n, c in enumerate((kv, pl.ds(0, channels)))]
    tails[0].start()
    par_cps = [pltpu.make_async_copy(a, b, par_sem.at[n]) for n, (a, b) in enumerate(
        ((rates_in, rate_n), (taps_in, taps_n), (resid_in, res_n), (skip_in, skip_v)))]
    par_cps[0].start()
    par_cps[1].start()

    def in_copy(f, g):
        cols = pl.ds(pl.multiple_of((f * groups + g) * GROUP, GROUP), GROUP)
        return pltpu.make_async_copy(proj.at[pl.ds(0, last), cols], raw.at[pl.ds(0, last), cols],
                                     in_sem.at[f * groups + g])

    for idx in range(groups):
        in_copy(1, far_first(idx)).start()
        in_copy(2, far_first(idx)).start()
    par_cps[2].start()
    par_cps[3].start()
    tails[1].start()
    for g in range(groups):
        in_copy(0, g).start()

    bar = pltpu.get_barrier_semaphore()
    nxt, prv = dev(lax.rem(p + 1, total)), dev(lax.rem(p + total - 1, total))
    for to in (nxt, prv):
        pl.semaphore_signal(bar, inc=1, device_id=to, device_id_type=MESH)
    for k in range(1, n2):
        pl.semaphore_signal(bar, inc=1, device_id=dev(lax.rem(h + k, n2) * n1 + e), device_id_type=MESH)
    for n in ring_order():
        pl.semaphore_signal(bar, inc=1, device_id=mate(n), device_id_type=MESH)

    def relay(dst, row, f, g, c):
        for s in range(SUB):
            col = pl.multiple_of((f * groups + g) * GROUP + s * LANE, LANE)
            v = raw[pl.ds(pl.multiple_of(c * CHUNK, CHUNK), CHUNK), pl.ds(col, LANE)].astype(F32)
            dst[pl.ds(row + s, CHUNK, stride=SUB), :] = v

    def tail_of(f):
        for g in range(groups):
            relay(ttmp.at[f * groups + g], 0, f, g, chunks - 1)
            hsend[f * groups + g] = ttmp[f * groups + g, pl.ds((CHUNK - 2) * SUB, 2 * SUB), :].astype(BF16)

    tails[0].wait()
    tail_of(1)
    tail_of(2)
    kv_blocks, q_blocks = pl.ds(groups, 2 * groups), pl.ds(0, groups)
    halo = remote(hsend.at[kv_blocks], hrecv.at[kv_blocks], hs_sem.at[0], hr_sem.at[0], nxt)
    halo_q = remote(hsend.at[q_blocks], hrecv.at[q_blocks], hs_sem.at[1], hr_sem.at[1], nxt)

    def send_rim():
        @pl.when(z == 0)
        def _():
            for g in range(groups):
                for n, f in enumerate((1, 2)):
                    relay(ktmp, 0, f, g, 0)
                    xstage[g, pl.ds(n * 2 * SUB, 2 * SUB), :] = ktmp[pl.ds(0, 2 * SUB), :]

        @pl.when(z != 0)
        def _():
            for g in range(groups):
                for n, f in enumerate((1, 2)):
                    xstage[g, pl.ds(n * 2 * SUB, 2 * SUB), :] = ttmp[f * groups + g, pl.ds((CHUNK - 2) * SUB, 2 * SUB), :]

        for g in range(groups):
            for t in range(SUB):
                xsend[g * SUB + t] = xstage[g, pl.ds(t, 4, stride=SUB), :].astype(BF16)
        slot = jnp.where(z == 0, hi, high + hi)

        def one(n, _):
            to = owner(n)

            @pl.when(to == e)
            def _():
                xrecv[slot] = xsend[n]

            @pl.when(to != e)
            def _():
                remote(xsend.at[n], xrecv.at[slot], xs_sem.at[n], xr_sem.at[slot], mate(to)).start()

            return 0

        lax.fori_loop(0, n1, one, 0)

    par_cps[0].wait()
    par_cps[1].wait()
    for f in (1, 2):
        for g in range(groups):
            fg = f * groups + g
            for s in range(SUB):
                taps_t[pl.ds(fg * 3 * SUB + s, 3, stride=SUB), :] = taps_n[:, pl.ds(fg * GROUP + s * LANE, LANE)]
    for g in range(groups):
        for s in range(SUB):
            rtm[g, pl.ds(s, modes, stride=SUB), :] = rate_n[:, pl.ds(g * GROUP + s * LANE, LANE)]
        r = rtm[g]
        dtm[g] = jnp.exp(-r)
        d16[g] = jnp.exp(-float(CHUNK) * r)

    def tap(f, g):
        return [taps_t[pl.ds(pl.multiple_of(((f * groups + g) * 3 + j) * SUB, SUB), SUB), :] for j in range(3)]

    def mode(ref, g, m):
        return ref[g, pl.ds(m * SUB, SUB), :]

    def at(t):
        return pl.ds(pl.multiple_of(t * SUB, SUB), SUB)

    def tree(vals):
        vals = list(vals)
        while len(vals) > 1:
            vals = [a + b for a, b in zip(vals[::2], vals[1::2])] + (vals[-1:] if len(vals) % 2 else [])
        return vals[0]

    zero = jnp.zeros((SUB, LANE), F32)

    def states(g):
        d = [mode(dtm, g, m) for m in range(modes)]
        tk, tv = tap(1, g), tap(2, g)
        relay(ktmp, 0, 1, g, 0)
        relay(vtmp, 0, 2, g, 0)
        head[g, pl.ds(0, 2 * SUB), :] = ktmp[pl.ds(0, 2 * SUB), :]
        head[g, pl.ds(2 * SUB, 2 * SUB), :] = vtmp[pl.ds(0, 2 * SUB), :]
        for m in range(modes):
            ztm[g, pl.ds(m * SUB, SUB), :] = zero

        def chunk(c, bufs, spare, carry):
            ahead = jnp.minimum(c + 1, chunks - 1)
            relay(spare[0], 0, 1, g, ahead)
            relay(spare[1], 0, 2, g, ahead)
            k1, k2, v1, v2 = carry
            u = [None] * modes
            for t in range(CHUNK):
                k0, v0 = bufs[0][pl.ds(t * SUB, SUB), :], bufs[1][pl.ds(t * SUB, SUB), :]
                x = (tk[0] * k0 + tk[1] * k1 + tk[2] * k2) * (tv[0] * v0 + tv[1] * v1 + tv[2] * v2)
                if t < 2:
                    x = jnp.where(c == 0, zero, x)
                k1, k2, v1, v2 = k0, k1, v0, v1
                xs[g, at(c * CHUNK + t), :] = x
                u = [x if u[m] is None else d[m] * u[m] + x for m in range(modes)]
            for m in range(modes):
                ends[g, at(c * modes + m), :] = u[m]
                ztm[g, pl.ds(m * SUB, SUB), :] = mode(d16, g, m) * mode(ztm, g, m) + u[m]
            return k1, k2, v1, v2

        def pair(j, carry):
            carry = chunk(2 * j, (ktmp, vtmp), (ktmp2, vtmp2), carry)
            return chunk(2 * j + 1, (ktmp2, vtmp2), (ktmp, vtmp), carry)

        lax.fori_loop(0, chunks // 2, pair, (zero, zero, zero, zero))

    first = p == 0

    def halo_of(f, g):
        both = hrecv[f * groups + g].astype(F32)
        both = jnp.where(first, jnp.zeros_like(both), both)
        return both[:SUB], both[SUB:]

    def edges(g):
        feats = []
        for n, f in enumerate((1, 2)):
            h2, h1 = halo_of(f, g)
            t0, t1, t2 = tap(f, g)
            e0, e1 = head[g, pl.ds(2 * n * SUB, SUB), :], head[g, pl.ds((2 * n + 1) * SUB, SUB), :]
            feats.append((t0 * e0 + t1 * h1 + t2 * h2, t0 * e1 + t1 * e0 + t2 * h1))
        edge[g, pl.ds(0, SUB), :] = feats[0][0] * feats[1][0]
        edge[g, pl.ds(SUB, SUB), :] = feats[0][1] * feats[1][1]

    def emit(g):
        @pl.when(near)
        def _():
            edges(g)

        @pl.when(jnp.logical_not(near))
        def _():
            edge[g] = jnp.zeros((2 * SUB, LANE), F32)

        x0, x1 = edge[g, pl.ds(0, SUB), :], edge[g, pl.ds(SUB, SUB), :]
        for m in range(modes):
            state = mode(ztm, g, m) + jnp.exp(-(rows - 2.0) * mode(rtm, g, m)) * (mode(dtm, g, m) * x0 + x1)
            stg[g, pl.ds(m, SUB, stride=modes), :] = state
        for s in range(SUB):
            send1[g * SUB + s] = stg[g, pl.ds(s * modes, modes), :].astype(BF16)
        for s in range(SUB):
            n, to = g * SUB + s, own_by(g, s)

            @pl.when(to == e)
            def _():
                recv1[e] = send1[n]

            @pl.when(to != e)
            def _():
                remote(send1.at[n], recv1.at[e], s1_sem.at[n], r1_sem.at[e], mate(to)).start()

    early = groups - 1
    for idx in range(groups):
        if idx < 2:
            for k in ((0,) if idx == 0 else range(1, groups)):
                for f in (1, 2):
                    in_copy(f, far_first(k)).wait()
        states(far_first(idx))
        if idx == (groups - 1) // 2:
            pl.semaphore_wait(bar, n1 + n2)
            halo.start()
            pl.when(rim)(send_rim)
        if idx == max(early - 1, 0):
            @pl.when(near)
            def _():
                halo.wait_recv()

            def emit_early(k, _):
                emit(far_first(k))
                return 0

            if early:
                lax.fori_loop(0, early, emit_early, 0)
    emit(far_first(groups - 1))

    tails[1].wait()
    tail_of(0)
    halo_q.start()
    par_cps[2].wait()
    par_cps[3].wait()
    for g in range(groups):
        for s in range(SUB):
            taps_t[pl.ds(g * 3 * SUB + s, 3, stride=SUB), :] = taps_n[:, pl.ds(g * GROUP + s * LANE, LANE)]
            cols = pl.ds(g * GROUP + s * LANE, LANE)
            atm[g, pl.ds(s, modes, stride=SUB), :] = res_n[:, cols] * jnp.sqrt(2.0 * rate_n[:, cols])
    for g in range(groups):
        in_copy(0, g).wait()
        t0, t1, t2 = tap(0, g)

        def gate(c, bufs, spare, carry):
            relay(spare, 0, 0, g, jnp.minimum(c + 1, chunks - 1))
            q1, q2 = carry
            for t in range(CHUNK):
                q0 = bufs[pl.ds(t * SUB, SUB), :]
                qtm[g, at(c * CHUNK + t), :] = t0 * q0 + t1 * q1 + t2 * q2
                q1, q2 = q0, q1
            return q1, q2

        def gates(j, carry):
            return gate(2 * j + 1, ktmp2, ktmp, gate(2 * j, ktmp, ktmp2, carry))

        relay(ktmp, 0, 0, g, 0)
        lax.fori_loop(0, chunks // 2, gates, (zero, zero))

    own_cols = pl.ds(pl.multiple_of(mine * LANE, LANE), LANE)
    own = rate_n[:, own_cols]
    dec_in = jnp.exp(-float(rows) * own)
    dec_out = jnp.exp(-float(rows * n1) * own)
    dec_one, dec_edge = jnp.exp(-own), jnp.exp(-(rows - 2.0) * own)
    own_taps = [taps_n[pl.ds(j, 1), pl.ds(pl.multiple_of(f * channels + mine * LANE, LANE), LANE)]
                for f in (1, 2) for j in range(3)]

    def rows_of(val):
        xwork[...] = val
        return [xwork[pl.ds(j, 1), :] for j in range(4)]

    def edge_state(heads, tails):
        ends_x = []
        for j in (0, 1):
            t0, t1, t2 = own_taps[3 * j:3 * j + 3]
            e0, e1, h2, h1 = heads[2 * j], heads[2 * j + 1], tails[2 * j], tails[2 * j + 1]
            ends_x.append((t0 * e0 + t1 * h1 + t2 * h2, t0 * e1 + t1 * e0 + t2 * h1))
        x0, x1 = ends_x[0][0] * ends_x[1][0], ends_x[0][1] * ends_x[1][1]
        return dec_edge * (dec_one * x0 + x1)

    for k in range(high):
        for slot, src in ((k, k * RING), (high + k, k * RING + RING - 1)):
            @pl.when(src != e)
            def _():
                remote(xsend.at[0], xrecv.at[slot], xs_sem.at[0], xr_sem.at[slot], mate(src)).wait_recv()
    fixes = [None] + [edge_state(rows_of(xrecv[k].astype(F32)), rows_of(xrecv[high + k - 1].astype(F32)))
                      for k in range(1, high)]
    send2[1, pl.ds(0, 8), :] = jnp.concatenate([xrecv[0].astype(F32), xrecv[2 * high - 1].astype(F32)], 0).astype(BF16)
    run = jnp.zeros((modes, LANE), F32)
    for n in range(n1):
        pre[n] = run

        @pl.when(n != e)
        def _():
            remote(send1.at[n], recv1.at[n], s1_sem.at[n], r1_sem.at[n], mate(n)).wait_recv()

        run = dec_in * run + recv1[n].astype(F32)
        if n % RING == 0 and n:
            run = run + fixes[n // RING]
    send2[0] = run.astype(BF16)
    for k in range(n2 - 1, 0, -1):
        @pl.when(h + k < n2)
        def _():
            remote(send2, recv2.at[h], s2_sem.at[k], r2_sem.at[h], dev((h + k) * n1 + e)).start()

    power = jnp.ones((modes, LANE), F32)
    for n in range(n1):
        powr[n] = power
        power = power * dec_in

    def local(g):
        d = [mode(dtm, g, m) for m in range(modes)]
        a = [mode(atm, g, m) for m in range(modes)]
        taps = []
        for j in range(CHUNK):
            taps.append(tree(a))
            a = [d[m] * a[m] for m in range(modes)]
        taps[0] = taps[0] + skip_v[pl.ds(g * SUB, SUB), :]

        def body(c, _):
            x = [xs[g, at(c * CHUNK + t), :] for t in range(CHUNK)]
            for t in range(CHUNK):
                base[g, at(c * CHUNK + t), :] = tree([taps[j] * x[t - j] for j in range(t + 1)])
            for m in range(modes):
                ends[g, at(c * modes + m), :] = mode(atm, g, m) * ends[g, at(c * modes + m), :]
            return 0

        lax.fori_loop(0, chunks, body, 0)

    def fix_edge(g):
        x0, x1 = edge[g, pl.ds(0, SUB), :], edge[g, pl.ds(SUB, SUB), :]
        sk = skip_v[pl.ds(g * SUB, SUB), :]
        lead = tree([mode(atm, g, m) * jnp.exp(mode(rtm, g, m)) for m in range(modes)])
        base[g, pl.ds(0, SUB), :] = sk * x0 - x1 * lead
        base[g, pl.ds(SUB, SUB), :] = sk * x1
        for m in range(modes):
            r = mode(rtm, g, m)
            ztm[g, pl.ds(m * SUB, SUB), :] = jnp.exp(r) * x0 + jnp.exp(2.0 * r) * x1

    split = (groups + 1) // 2
    for g in range(split):
        local(g)

    def add_outer(n, carry):
        acc, tails = carry[0], carry[1:]
        remote(send2, recv2.at[n], s2_sem.at[0], r2_sem.at[n], dev(n * n1 + e)).wait_recv()
        xwork2[...] = recv2[n, 1, pl.ds(0, 8), :].astype(F32)
        both = [xwork2[pl.ds(j, 1), :] for j in range(8)]
        whole = recv2[n, 0].astype(F32) + last_power * edge_state(both[:4], tails)
        return (dec_out * acc + whole, *both[4:])

    last_power = powr[n1 - 1]
    none = jnp.zeros((1, LANE), F32)
    done = lax.fori_loop(0, h, add_outer, (jnp.zeros((modes, LANE), F32), none, none, none, none))
    carried = done[0]
    after = dec_in * carried + edge_state(rows_of(xrecv[0].astype(F32)), done[1:])
    send3[0] = carried.astype(BF16)
    for n in range(1, n1):
        send3[n] = (pre[n] + powr[n - 1] * after).astype(BF16)
    recv3[mine] = send3[e]
    for n in ring_order():
        remote(send3.at[n], recv3.at[mine], s3_sem.at[n], r3_sem.at[mine], mate(n)).start()
    for g in range(split, groups):
        local(g)

    @pl.when(jnp.logical_not(near))
    def _():
        halo.wait_recv()
        for g in range(groups):
            edges(g)

    for g in range(groups):
        fix_edge(g)
    halo_q.wait_recv()
    for g in range(groups):
        h2, h1 = halo_of(0, g)
        t0, t1, t2 = tap(0, g)
        qtm[g, pl.ds(0, SUB), :] = qtm[g, pl.ds(0, SUB), :] + (t1 * h1 + t2 * h2)
        qtm[g, pl.ds(SUB, SUB), :] = qtm[g, pl.ds(SUB, SUB), :] + t2 * h1

    for idx in range(groups - 1, -1, -1):
        g = far_first(idx)
        for s in range(SUB):
            n, src = g * SUB + s, own_by(g, s)

            @pl.when(src != e)
            def _():
                remote(send3.at[n], recv3.at[n], s3_sem.at[n], r3_sem.at[n], mate(src)).wait_recv()

            ctm[g, pl.ds(s, modes, stride=SUB), :] = recv3[n].astype(F32)
        d = [mode(dtm, g, m) for m in range(modes)]
        init = tuple(mode(atm, g, m) * (mode(ctm, g, m) + mode(ztm, g, m)) for m in range(modes))

        def apply(c, buf, carry):
            s = list(carry)
            for t in range(CHUNK):
                s = [d[m] * s[m] for m in range(modes)]
                here = at(c * CHUNK + t)
                buf[pl.ds(t * SUB, SUB), :] = qtm[g, here, :] * (base[g, here, :] + tree(s))
            for w in range(SUB):
                v = buf[pl.ds(w, CHUNK, stride=SUB), :].astype(BF16)
                cols = pl.ds(pl.multiple_of(g * GROUP + w * LANE, LANE), LANE)
                out[pl.ds(pl.multiple_of(c * CHUNK, CHUNK), CHUNK), cols] = v
            return tuple(s[m] + ends[g, at(c * modes + m), :] for m in range(modes))

        def applies(j, carry):
            return apply(2 * j + 1, ytmp2, apply(2 * j, ytmp, carry))

        lax.fori_loop(0, chunks // 2, applies, init)

    halo.wait_send()
    halo_q.wait_send()

    def drain(n, _):
        @pl.when(n != mine)
        def _():
            remote(send1.at[n], send1.at[n], s1_sem.at[n], s1_sem.at[n], nxt).wait_send()

        @pl.when(n != e)
        def _():
            remote(send3.at[n], send3.at[n], s3_sem.at[n], s3_sem.at[n], nxt).wait_send()

        @pl.when(jnp.logical_and(rim, n != mine))
        def _():
            remote(xsend.at[n], xsend.at[n], xs_sem.at[n], xs_sem.at[n], nxt).wait_send()

        return 0

    lax.fori_loop(0, n1, drain, 0)
    for k in range(1, n2):
        @pl.when(h + k < n2)
        def _():
            remote(send2, send2, s2_sem.at[k], s2_sem.at[k], nxt).wait_send()


def solution(mesh):
    outer_n, inner_n = mesh.shape["outer"], mesh.shape["inner"]

    def on_device(projected, short_taps, rates, residues, skip_gain):
        rows, width = projected.shape
        channels, modes = rates.shape
        groups = channels // GROUP
        n1 = channels // LANE
        n2 = outer_n * inner_n // n1
        any_spec = pl.BlockSpec(memory_space=pl.ANY)
        dma = pltpu.SemaphoreType.DMA
        tm = pltpu.VMEM((groups, rows * SUB, LANE), F32)
        pm = pltpu.VMEM((groups, modes * SUB, LANE), F32)
        tmp = pltpu.VMEM((CHUNK * SUB, LANE), F32)
        msg = pltpu.VMEM((n1, modes, LANE), BF16)
        return pl.pallas_call(
            functools.partial(kernel, (outer_n, inner_n, rows, channels, modes)),
            out_shape=pltpu.VMEM((rows, channels), BF16),
            in_specs=[any_spec] * 5,
            out_specs=pl.BlockSpec(memory_space=pltpu.VMEM),
            scratch_shapes=[
                pltpu.VMEM((rows, width), BF16), tmp, tmp, tmp, tmp,
                pltpu.VMEM((3 * groups, CHUNK * SUB, LANE), F32), tm, tm, tm,
                pltpu.VMEM((3, width), F32), pltpu.VMEM((modes, channels), F32), pltpu.VMEM((modes, channels), F32),
                pltpu.VMEM((groups * SUB, LANE), F32), pltpu.VMEM((3 * 3 * groups * SUB, LANE), F32),
                pm, pm, pm, pm, pm,
                pltpu.VMEM((groups, rows // CHUNK * modes * SUB, LANE), F32),
                pltpu.VMEM((groups, 2 * SUB, LANE), F32), pltpu.VMEM((groups, 4 * SUB, LANE), F32),
                pm, pm,
                pltpu.VMEM((n1, modes, LANE), F32), pltpu.VMEM((n1, modes, LANE), F32),
                pltpu.VMEM((3 * groups, 2 * SUB, LANE), BF16), pltpu.VMEM((3 * groups, 2 * SUB, LANE), BF16),
                pltpu.VMEM((groups, 4 * SUB, LANE), F32), pltpu.VMEM((4, LANE), F32), pltpu.VMEM((8, LANE), F32),
                pltpu.VMEM((n1, 4, LANE), BF16), pltpu.VMEM((2 * n1 // RING, 4, LANE), BF16),
                msg, msg, pltpu.VMEM((2, modes, LANE), BF16), pltpu.VMEM((n2, 2, modes, LANE), BF16), msg, msg,
                tmp, tmp,
                dma((3 * groups + 2,)), dma((4,)), dma((2,)), dma((2,)), dma((n1,)), dma((2 * n1 // RING,)),
                dma((n1,)), dma((n1,)), dma((n2,)), dma((n2,)), dma((n1,)), dma((n1,)),
            ],
            compiler_params=pltpu.CompilerParams(collective_id=0, has_side_effects=True,
                                                 vmem_limit_bytes=60 * 1024 * 1024),
            name="modal_scan",
        )(projected, short_taps, rates.T, residues.T, skip_gain.reshape(groups * SUB, LANE))

    return jax.shard_map(
        on_device, mesh=mesh,
        in_specs=(P(("outer", "inner"), None), P(), P(), P(), P()),
        out_specs=P(("outer", "inner"), None), check_vma=False,
    )
```

```python
import functools

import jax
import jax.numpy as jnp
from jax import lax
from jax.experimental import pallas as pl
from jax.experimental.pallas import tpu as pltpu
from jax.sharding import PartitionSpec as P

MESH = pl.DeviceIdType.MESH
F32 = jnp.float32
BF16 = jnp.bfloat16
SUB = 8
LANE = 128
GROUP = SUB * LANE
CHUNK = 16
RING = 8


def kernel(dims, proj, taps_in, rates_in, resid_in, skip_in, out, raw, ktmp, vtmp, ktmp2, vtmp2, ttmp, qtm, xs, base, taps_n,
           rate_n, res_n, skip_v, taps_t, rtm, dtm, d16, atm, ztm, ends, edge, head, stg, ctm, pre, powr, hsend, hrecv, xwork,
           send1, recv1, send2, recv2, send3, recv3, ytmp, ytmp2, in_sem, par_sem, hs_sem, hr_sem,
           s1_sem, r1_sem, s2_sem, r2_sem, s3_sem, r3_sem):
    outer_n, inner_n, rows, channels, modes = dims
    groups = channels // GROUP
    chunks = rows // CHUNK
    n1 = channels // LANE
    total = outer_n * inner_n
    n2 = total // n1
    last = rows - CHUNK
    p = lax.axis_index("outer") * inner_n + lax.axis_index("inner")
    e = lax.rem(p, n1)
    h = p // n1
    z = lax.rem(e, RING)
    hi = e // RING
    zpg = RING // groups
    late = z >= RING // 2
    mine = (z // zpg) * SUB + hi * zpg + lax.rem(z, zpg)

    def far_first(idx):
        if groups == 1:
            return 0
        odd = lax.rem(z, 2)
        off = (2, 1 + 2 * odd, 3 - 2 * odd, 0)
        step = off[idx] if isinstance(idx, int) else jnp.where(
            idx == 0, off[0], jnp.where(idx == 1, off[1], jnp.where(idx == 2, off[2], off[3])))
        return lax.rem(z // zpg + step, groups)

    def own_by(g, s):
        return (s // zpg) * RING + zpg * g + s % zpg

    def dev(r):
        return (r // inner_n, lax.rem(r, inner_n))

    def mate(n):
        return dev(h * n1 + n)

    def ring_order():
        for dz in (4, 3, 5, 2, 6, 1, 7, 0):
            for hi in range(n1 // RING):
                if dz or hi:
                    yield lax.rem(e // RING + hi, n1 // RING) * RING + lax.rem(lax.rem(e, RING) + dz, RING)

    def remote(src, dst, ssem, rsem, to):
        return pltpu.make_async_remote_copy(src_ref=src, dst_ref=dst, send_sem=ssem, recv_sem=rsem, device_id=to,
                                            device_id_type=MESH)

    kv = pl.ds(channels, 2 * channels)
    tails = [pltpu.make_async_copy(proj.at[pl.ds(last, CHUNK), c], raw.at[pl.ds(last, CHUNK), c], in_sem.at[3 * groups + n])
             for n, c in enumerate((kv, pl.ds(0, channels)))]
    tails[0].start()
    par_cps = [pltpu.make_async_copy(a, b, par_sem.at[n]) for n, (a, b) in enumerate(
        ((rates_in, rate_n), (taps_in, taps_n), (resid_in, res_n), (skip_in, skip_v)))]
    par_cps[0].start()
    par_cps[1].start()

    def in_copy(f, g):
        cols = pl.ds(pl.multiple_of((f * groups + g) * GROUP, GROUP), GROUP)
        return pltpu.make_async_copy(proj.at[pl.ds(0, last), cols], raw.at[pl.ds(0, last), cols],
                                     in_sem.at[f * groups + g])

    for idx in range(groups):
        in_copy(1, far_first(idx)).start()
        in_copy(2, far_first(idx)).start()
    par_cps[2].start()
    par_cps[3].start()
    tails[1].start()
    for g in range(groups):
        in_copy(0, g).start()

    bar = pltpu.get_barrier_semaphore()
    nxt, prv = dev(lax.rem(p + 1, total)), dev(lax.rem(p + total - 1, total))
    for to in (nxt, prv):
        pl.semaphore_signal(bar, inc=1, device_id=to, device_id_type=MESH)
    for k in range(1, n2):
        pl.semaphore_signal(bar, inc=1, device_id=dev(lax.rem(h + k, n2) * n1 + e), device_id_type=MESH)
    for n in ring_order():
        pl.semaphore_signal(bar, inc=1, device_id=mate(n), device_id_type=MESH)

    def relay(dst, row, f, g, c):
        for s in range(SUB):
            col = pl.multiple_of((f * groups + g) * GROUP + s * LANE, LANE)
            v = raw[pl.ds(pl.multiple_of(c * CHUNK, CHUNK), CHUNK), pl.ds(col, LANE)].astype(F32)
            dst[pl.ds(row + s, CHUNK, stride=SUB), :] = v

    def tail_of(f):
        for g in range(groups):
            relay(ttmp.at[g], 0, f, g, chunks - 1)
            tail = ttmp[g, pl.ds((CHUNK - 2) * SUB, 2 * SUB), :]
            hsend[f * groups + g] = tail.astype(BF16)
            if f:
                head[g, pl.ds((2 + 2 * f) * SUB, 2 * SUB), :] = tail

    tails[0].wait()
    tail_of(1)
    tail_of(2)
    halo = remote(hsend, hrecv, hs_sem, hr_sem, nxt)

    par_cps[0].wait()
    par_cps[1].wait()
    for f in (1, 2):
        for g in range(groups):
            fg = f * groups + g
            for s in range(SUB):
                taps_t[pl.ds(fg * 3 * SUB + s, 3, stride=SUB), :] = taps_n[:, pl.ds(fg * GROUP + s * LANE, LANE)]
    for g in range(groups):
        for s in range(SUB):
            rtm[g, pl.ds(s, modes, stride=SUB), :] = rate_n[:, pl.ds(g * GROUP + s * LANE, LANE)]
        r = rtm[g]
        dtm[g] = jnp.exp(-r)
        d16[g] = jnp.exp(-float(CHUNK) * r)

    def tap(f, g):
        return [taps_t[pl.ds(pl.multiple_of(((f * groups + g) * 3 + j) * SUB, SUB), SUB), :] for j in range(3)]

    def mode(ref, g, m):
        return ref[g, pl.ds(m * SUB, SUB), :]

    def at(t):
        return pl.ds(pl.multiple_of(t * SUB, SUB), SUB)

    def tree(vals):
        vals = list(vals)
        while len(vals) > 1:
            vals = [a + b for a, b in zip(vals[::2], vals[1::2])] + (vals[-1:] if len(vals) % 2 else [])
        return vals[0]

    zero = jnp.zeros((SUB, LANE), F32)

    def states(g):
        d = [mode(dtm, g, m) for m in range(modes)]
        tk, tv = tap(1, g), tap(2, g)
        relay(ktmp, 0, 1, g, 0)
        relay(vtmp, 0, 2, g, 0)
        head[g, pl.ds(0, 2 * SUB), :] = ktmp[pl.ds(0, 2 * SUB), :]
        head[g, pl.ds(2 * SUB, 2 * SUB), :] = vtmp[pl.ds(0, 2 * SUB), :]
        for m in range(modes):
            ztm[g, pl.ds(m * SUB, SUB), :] = zero

        def chunk(c, bufs, spare, carry):
            ahead = jnp.minimum(c + 1, chunks - 1)
            relay(spare[0], 0, 1, g, ahead)
            relay(spare[1], 0, 2, g, ahead)
            k1, k2, v1, v2 = carry
            u = [None] * modes
            for t in range(CHUNK):
                k0, v0 = bufs[0][pl.ds(t * SUB, SUB), :], bufs[1][pl.ds(t * SUB, SUB), :]
                x = (tk[0] * k0 + tk[1] * k1 + tk[2] * k2) * (tv[0] * v0 + tv[1] * v1 + tv[2] * v2)
                if t < 2:
                    x = jnp.where(c == 0, zero, x)
                k1, k2, v1, v2 = k0, k1, v0, v1
                xs[g, at(c * CHUNK + t), :] = x
                u = [x if u[m] is None else d[m] * u[m] + x for m in range(modes)]
            for m in range(modes):
                ends[g, at(c * modes + m), :] = u[m]
                ztm[g, pl.ds(m * SUB, SUB), :] = mode(d16, g, m) * mode(ztm, g, m) + u[m]
            return k1, k2, v1, v2

        def pair(j, carry):
            carry = chunk(2 * j, (ktmp, vtmp), (ktmp2, vtmp2), carry)
            return chunk(2 * j + 1, (ktmp2, vtmp2), (ktmp, vtmp), carry)

        lax.fori_loop(0, chunks // 2, pair, (zero, zero, zero, zero))

    first = p == 0

    def halo_of(f, g):
        both = hrecv[f * groups + g].astype(F32)
        both = jnp.where(first, jnp.zeros_like(both), both)
        return both[:SUB], both[SUB:]

    def edges(g):
        feats = []
        for n, f in enumerate((1, 2)):
            h2, h1 = halo_of(f, g)
            t0, t1, t2 = tap(f, g)
            e0, e1 = head[g, pl.ds(2 * n * SUB, SUB), :], head[g, pl.ds((2 * n + 1) * SUB, SUB), :]
            feats.append((t0 * e0 + t1 * h1 + t2 * h2, t0 * e1 + t1 * e0 + t2 * h1))
        edge[g, pl.ds(0, SUB), :] = feats[0][0] * feats[1][0]
        edge[g, pl.ds(SUB, SUB), :] = feats[0][1] * feats[1][1]

    def emit(g):
        for m in range(modes):
            stg[g, pl.ds(m, SUB, stride=modes), :] = mode(ztm, g, m)
        for s in range(SUB):
            send1[g * SUB + s, pl.ds(0, modes), :] = stg[g, pl.ds(s * modes, modes), :].astype(BF16)
            send1[g * SUB + s, pl.ds(modes, SUB), :] = head[g, pl.ds(s, SUB, stride=SUB), :].astype(BF16)
        for s in range(SUB):
            n, to = g * SUB + s, own_by(g, s)

            @pl.when(to == e)
            def _():
                recv1[e] = send1[n]

            @pl.when(to != e)
            def _():
                remote(send1.at[n], recv1.at[e], s1_sem.at[n], r1_sem.at[e], mate(to)).start()

    def emit_all(k, _):
        emit(far_first(k))
        return 0

    half = min(2, groups - 1)
    for idx in range(groups):
        if idx < 2:
            for k in ((0,) if idx == 0 else range(1, groups)):
                for f in (1, 2):
                    in_copy(f, far_first(k)).wait()
        states(far_first(idx))
        if idx == half - 1:
            @pl.when(late)
            def _():
                pl.semaphore_wait(bar, n1 + n2)
                lax.fori_loop(0, half, emit_all, 0)
        elif half <= idx < groups - 1:
            @pl.when(late)
            def _():
                emit(far_first(idx))

    if half:
        @pl.when(jnp.logical_not(late))
        def _():
            pl.semaphore_wait(bar, n1 + n2)
            lax.fori_loop(0, groups - 1, emit_all, 0)
    else:
        pl.semaphore_wait(bar, n1 + n2)
    emit(far_first(groups - 1))

    tails[1].wait()
    tail_of(0)
    halo.start()
    par_cps[2].wait()
    par_cps[3].wait()
    for g in range(groups):
        for s in range(SUB):
            taps_t[pl.ds(g * 3 * SUB + s, 3, stride=SUB), :] = taps_n[:, pl.ds(g * GROUP + s * LANE, LANE)]
            cols = pl.ds(g * GROUP + s * LANE, LANE)
            atm[g, pl.ds(s, modes, stride=SUB), :] = res_n[:, cols] * jnp.sqrt(2.0 * rate_n[:, cols])
    for g in range(groups):
        in_copy(0, g).wait()
        t0, t1, t2 = tap(0, g)

        def gate(c, bufs, spare, carry):
            relay(spare, 0, 0, g, jnp.minimum(c + 1, chunks - 1))
            q1, q2 = carry
            for t in range(CHUNK):
                q0 = bufs[pl.ds(t * SUB, SUB), :]
                qtm[g, at(c * CHUNK + t), :] = t0 * q0 + t1 * q1 + t2 * q2
                q1, q2 = q0, q1
            return q1, q2

        def gates(j, carry):
            return gate(2 * j + 1, ktmp2, ktmp, gate(2 * j, ktmp, ktmp2, carry))

        relay(ktmp, 0, 0, g, 0)
        lax.fori_loop(0, chunks // 2, gates, (zero, zero))

    own_cols = pl.ds(pl.multiple_of(mine * LANE, LANE), LANE)
    own = rate_n[:, own_cols]
    dec_in = jnp.exp(-float(rows) * own)
    dec_out = jnp.exp(-float(rows * n1) * own)
    dec_one, dec_edge = jnp.exp(-own), jnp.exp(-(rows - 2.0) * own)
    own_taps = [taps_n[pl.ds(j, 1), pl.ds(pl.multiple_of(f * channels + mine * LANE, LANE), LANE)]
                for f in (1, 2) for j in range(3)]

    def row(base_row, j):
        return xwork[pl.ds(base_row + j, 1), :]

    def edge_state(heads, tails):
        ends_x = []
        for j in (0, 1):
            t0, t1, t2 = own_taps[3 * j:3 * j + 3]
            e0, e1, h2, h1 = heads[2 * j], heads[2 * j + 1], tails[2 * j], tails[2 * j + 1]
            ends_x.append((t0 * e0 + t1 * h1 + t2 * h2, t0 * e1 + t1 * e0 + t2 * h1))
        x0, x1 = ends_x[0][0] * ends_x[1][0], ends_x[0][1] * ends_x[1][1]
        return dec_edge * (dec_one * x0 + x1)

    run = jnp.zeros((modes, LANE), F32)
    for n in range(n1):
        pre[n] = run

        @pl.when(n != e)
        def _():
            remote(send1.at[n], recv1.at[n], s1_sem.at[n], r1_sem.at[n], mate(n)).wait_recv()

        run = dec_in * run + recv1[n, pl.ds(0, modes), :].astype(F32)
        xwork[pl.ds(n * SUB, SUB), :] = recv1[n, pl.ds(modes, SUB), :].astype(F32)
        if n:
            run = run + edge_state([row(n * SUB, j) for j in range(4)], [row((n - 1) * SUB + 4, j) for j in range(4)])
    rim = [xwork[pl.ds(0, 4), :], xwork[pl.ds((n1 - 1) * SUB + 4, 4), :]]
    send2[1, pl.ds(0, 8), :] = jnp.concatenate(rim, 0).astype(BF16)
    send2[0] = run.astype(BF16)
    for k in range(n2 - 1, 0, -1):
        @pl.when(h + k < n2)
        def _():
            remote(send2, recv2.at[h], s2_sem.at[k], r2_sem.at[h], dev((h + k) * n1 + e)).start()

    power = jnp.ones((modes, LANE), F32)
    for n in range(n1):
        powr[n] = power
        power = power * dec_in

    def local(g):
        d = [mode(dtm, g, m) for m in range(modes)]
        a = [mode(atm, g, m) for m in range(modes)]
        taps = []
        for j in range(CHUNK):
            taps.append(tree(a))
            a = [d[m] * a[m] for m in range(modes)]
        taps[0] = taps[0] + skip_v[pl.ds(g * SUB, SUB), :]

        def body(c, _):
            x = [xs[g, at(c * CHUNK + t), :] for t in range(CHUNK)]
            for t in range(CHUNK):
                base[g, at(c * CHUNK + t), :] = tree([taps[j] * x[t - j] for j in range(t + 1)])
            for m in range(modes):
                ends[g, at(c * modes + m), :] = mode(atm, g, m) * ends[g, at(c * modes + m), :]
            return 0

        lax.fori_loop(0, chunks, body, 0)

    def fix_edge(g):
        x0, x1 = edge[g, pl.ds(0, SUB), :], edge[g, pl.ds(SUB, SUB), :]
        sk = skip_v[pl.ds(g * SUB, SUB), :]
        lead = tree([mode(atm, g, m) * jnp.exp(mode(rtm, g, m)) for m in range(modes)])
        base[g, pl.ds(0, SUB), :] = sk * x0 - x1 * lead
        base[g, pl.ds(SUB, SUB), :] = sk * x1
        for m in range(modes):
            r = mode(rtm, g, m)
            ztm[g, pl.ds(m * SUB, SUB), :] = jnp.exp(r) * x0 + jnp.exp(2.0 * r) * x1

    split = (groups + 1) // 2
    for g in range(split):
        local(g)

    def add_outer(n, carry):
        acc, tails = carry[0], carry[1:]
        remote(send2, recv2.at[n], s2_sem.at[0], r2_sem.at[n], dev(n * n1 + e)).wait_recv()
        xwork[pl.ds(n1 * SUB, SUB), :] = recv2[n, 1, pl.ds(0, 8), :].astype(F32)
        both = [row(n1 * SUB, j) for j in range(8)]
        whole = recv2[n, 0].astype(F32) + last_power * edge_state(both[:4], tails)
        return (dec_out * acc + whole, *both[4:])

    last_power = powr[n1 - 1]
    none = jnp.zeros((1, LANE), F32)
    done = lax.fori_loop(0, h, add_outer, (jnp.zeros((modes, LANE), F32), none, none, none, none))
    carried = done[0]
    after = dec_in * carried + edge_state([row(0, j) for j in range(4)], done[1:])
    send3[0] = carried.astype(BF16)
    for n in range(1, n1):
        send3[n] = (pre[n] + powr[n - 1] * after).astype(BF16)
    recv3[mine] = send3[e]
    for n in ring_order():
        remote(send3.at[n], recv3.at[mine], s3_sem.at[n], r3_sem.at[mine], mate(n)).start()
    for g in range(split, groups):
        local(g)
    halo.wait_recv()
    for g in range(groups):
        edges(g)
        fix_edge(g)
    for g in range(groups):
        h2, h1 = halo_of(0, g)
        t0, t1, t2 = tap(0, g)
        qtm[g, pl.ds(0, SUB), :] = qtm[g, pl.ds(0, SUB), :] + (t1 * h1 + t2 * h2)
        qtm[g, pl.ds(SUB, SUB), :] = qtm[g, pl.ds(SUB, SUB), :] + t2 * h1

    for idx in range(groups - 1, -1, -1):
        g = far_first(idx)
        for s in range(SUB):
            n, src = g * SUB + s, own_by(g, s)

            @pl.when(src != e)
            def _():
                remote(send3.at[n], recv3.at[n], s3_sem.at[n], r3_sem.at[n], mate(src)).wait_recv()

            ctm[g, pl.ds(s, modes, stride=SUB), :] = recv3[n].astype(F32)
        d = [mode(dtm, g, m) for m in range(modes)]
        init = tuple(mode(atm, g, m) * (mode(ctm, g, m) + mode(ztm, g, m)) for m in range(modes))

        def apply(c, buf, carry):
            s = list(carry)
            for t in range(CHUNK):
                s = [d[m] * s[m] for m in range(modes)]
                here = at(c * CHUNK + t)
                buf[pl.ds(t * SUB, SUB), :] = qtm[g, here, :] * (base[g, here, :] + tree(s))
            for w in range(SUB):
                v = buf[pl.ds(w, CHUNK, stride=SUB), :].astype(BF16)
                cols = pl.ds(pl.multiple_of(g * GROUP + w * LANE, LANE), LANE)
                out[pl.ds(pl.multiple_of(c * CHUNK, CHUNK), CHUNK), cols] = v
            return tuple(s[m] + ends[g, at(c * modes + m), :] for m in range(modes))

        def applies(j, carry):
            return apply(2 * j + 1, ytmp2, apply(2 * j, ytmp, carry))

        lax.fori_loop(0, chunks // 2, applies, init)

    halo.wait_send()

    def drain(n, _):
        @pl.when(n != mine)
        def _():
            remote(send1.at[n], send1.at[n], s1_sem.at[n], s1_sem.at[n], nxt).wait_send()

        @pl.when(n != e)
        def _():
            remote(send3.at[n], send3.at[n], s3_sem.at[n], s3_sem.at[n], nxt).wait_send()

        return 0

    lax.fori_loop(0, n1, drain, 0)
    for k in range(1, n2):
        @pl.when(h + k < n2)
        def _():
            remote(send2, send2, s2_sem.at[k], s2_sem.at[k], nxt).wait_send()


def solution(mesh):
    outer_n, inner_n = mesh.shape["outer"], mesh.shape["inner"]

    def on_device(projected, short_taps, rates, residues, skip_gain):
        rows, width = projected.shape
        channels, modes = rates.shape
        groups = channels // GROUP
        n1 = channels // LANE
        n2 = outer_n * inner_n // n1
        any_spec = pl.BlockSpec(memory_space=pl.ANY)
        dma = pltpu.SemaphoreType.DMA
        tm = pltpu.VMEM((groups, rows * SUB, LANE), F32)
        pm = pltpu.VMEM((groups, modes * SUB, LANE), F32)
        tmp = pltpu.VMEM((CHUNK * SUB, LANE), F32)
        msg = pltpu.VMEM((n1, modes, LANE), BF16)
        first_msg = pltpu.VMEM((n1, modes + SUB, LANE), BF16)
        return pl.pallas_call(
            functools.partial(kernel, (outer_n, inner_n, rows, channels, modes)),
            out_shape=pltpu.VMEM((rows, channels), BF16),
            in_specs=[any_spec] * 5,
            out_specs=pl.BlockSpec(memory_space=pltpu.VMEM),
            scratch_shapes=[
                pltpu.VMEM((rows, width), BF16), tmp, tmp, tmp, tmp,
                pltpu.VMEM((groups, CHUNK * SUB, LANE), F32), tm, tm, tm,
                pltpu.VMEM((3, width), F32), pltpu.VMEM((modes, channels), F32), pltpu.VMEM((modes, channels), F32),
                pltpu.VMEM((groups * SUB, LANE), F32), pltpu.VMEM((3 * 3 * groups * SUB, LANE), F32),
                pm, pm, pm, pm, pm,
                pltpu.VMEM((groups, rows // CHUNK * modes * SUB, LANE), F32),
                pltpu.VMEM((groups, 2 * SUB, LANE), F32), pltpu.VMEM((groups, 8 * SUB, LANE), F32),
                pm, pm,
                pltpu.VMEM((n1, modes, LANE), F32), pltpu.VMEM((n1, modes, LANE), F32),
                pltpu.VMEM((3 * groups, 2 * SUB, LANE), BF16), pltpu.VMEM((3 * groups, 2 * SUB, LANE), BF16),
                pltpu.VMEM(((n1 + 1) * SUB, LANE), F32), first_msg, first_msg,
                pltpu.VMEM((2, modes, LANE), BF16), pltpu.VMEM((n2, 2, modes, LANE), BF16), msg, msg,
                tmp, tmp,
                dma((3 * groups + 2,)), dma((4,)), dma, dma,
                dma((n1,)), dma((n1,)), dma((n2,)), dma((n2,)), dma((n1,)), dma((n1,)),
            ],
            compiler_params=pltpu.CompilerParams(collective_id=0, has_side_effects=True,
                                                 vmem_limit_bytes=60 * 1024 * 1024),
            name="modal_scan",
        )(projected, short_taps, rates.T, residues.T, skip_gain.reshape(groups * SUB, LANE))

    return jax.shard_map(
        on_device, mesh=mesh,
        in_specs=(P(("outer", "inner"), None), P(), P(), P(), P()),
        out_specs=P(("outer", "inner"), None), check_vma=False,
    )
```

```python
import functools

import jax
import jax.numpy as jnp
from jax import lax
from jax.experimental import pallas as pl
from jax.experimental.pallas import tpu as pltpu
from jax.sharding import PartitionSpec as P

MESH = pl.DeviceIdType.MESH
F32 = jnp.float32
BF16 = jnp.bfloat16
SUB = 8
LANE = 128
GROUP = SUB * LANE
CHUNK = 16
RING = 8


def kernel(dims, proj, taps_in, rates_in, resid_in, skip_in, out, raw, ktmp, vtmp, ktmp2, vtmp2, ttmp, qtm, xs, base, taps_n,
           rate_n, res_n, skip_v, taps_t, rtm, dtm, d16, atm, ztm, ends, edge, head, stg, ctm, pre, powr, hsend, hrecv, xwork,
           send1, recv1, send2, recv2, send3, recv3, ytmp, ytmp2, in_sem, par_sem, hs_sem, hr_sem,
           s1_sem, r1_sem, s2_sem, r2_sem, s3_sem, r3_sem):
    outer_n, inner_n, rows, channels, modes = dims
    groups = channels // GROUP
    chunks = rows // CHUNK
    n1 = channels // LANE
    total = outer_n * inner_n
    n2 = total // n1
    last = rows - CHUNK
    p = lax.axis_index("outer") * inner_n + lax.axis_index("inner")
    e = lax.rem(p, n1)
    h = p // n1
    z = lax.rem(e, RING)
    hi = e // RING
    zpg = RING // groups
    late = z >= RING // 2
    mine = (z // zpg) * SUB + hi * zpg + lax.rem(z, zpg)

    def far_first(idx):
        if groups == 1:
            return 0
        odd = lax.rem(z, 2)
        off = (2, 1 + 2 * odd, 3 - 2 * odd, 0)
        step = off[idx] if isinstance(idx, int) else jnp.where(
            idx == 0, off[0], jnp.where(idx == 1, off[1], jnp.where(idx == 2, off[2], off[3])))
        return lax.rem(z // zpg + step, groups)

    def own_by(g, s):
        return (s // zpg) * RING + zpg * g + s % zpg

    def dev(r):
        return (r // inner_n, lax.rem(r, inner_n))

    def mate(n):
        return dev(h * n1 + n)

    def ring_order():
        for dz in (4, 3, 5, 2, 6, 1, 7, 0):
            for hi in range(n1 // RING):
                if dz or hi:
                    yield lax.rem(e // RING + hi, n1 // RING) * RING + lax.rem(lax.rem(e, RING) + dz, RING)

    def remote(src, dst, ssem, rsem, to):
        return pltpu.make_async_remote_copy(src_ref=src, dst_ref=dst, send_sem=ssem, recv_sem=rsem, device_id=to,
                                            device_id_type=MESH)

    bar = pltpu.get_barrier_semaphore()
    nxt, prv = dev(lax.rem(p + 1, total)), dev(lax.rem(p + total - 1, total))
    for n in ring_order():
        pl.semaphore_signal(bar, inc=1, device_id=mate(n), device_id_type=MESH)
    for to in (nxt, prv):
        pl.semaphore_signal(bar, inc=1, device_id=to, device_id_type=MESH)
    for k in range(1, n2):
        pl.semaphore_signal(bar, inc=1, device_id=dev(lax.rem(h + k, n2) * n1 + e), device_id_type=MESH)

    kv = pl.ds(channels, 2 * channels)
    tails = [pltpu.make_async_copy(proj.at[pl.ds(last, CHUNK), c], raw.at[pl.ds(last, CHUNK), c], in_sem.at[3 * groups + n])
             for n, c in enumerate((kv, pl.ds(0, channels)))]
    tails[0].start()
    par_cps = [pltpu.make_async_copy(a, b, par_sem.at[n]) for n, (a, b) in enumerate(
        ((rates_in, rate_n), (taps_in, taps_n), (resid_in, res_n), (skip_in, skip_v)))]
    par_cps[0].start()
    par_cps[1].start()

    def in_copy(f, g):
        cols = pl.ds(pl.multiple_of((f * groups + g) * GROUP, GROUP), GROUP)
        return pltpu.make_async_copy(proj.at[pl.ds(0, last), cols], raw.at[pl.ds(0, last), cols],
                                     in_sem.at[f * groups + g])

    for idx in range(groups):
        in_copy(1, far_first(idx)).start()
        in_copy(2, far_first(idx)).start()
    par_cps[2].start()
    par_cps[3].start()
    tails[1].start()
    for g in range(groups):
        in_copy(0, g).start()

    def relay(dst, row, f, g, c):
        for s in range(SUB):
            col = pl.multiple_of((f * groups + g) * GROUP + s * LANE, LANE)
            v = raw[pl.ds(pl.multiple_of(c * CHUNK, CHUNK), CHUNK), pl.ds(col, LANE)].astype(F32)
            dst[pl.ds(row + s, CHUNK, stride=SUB), :] = v

    def tail_of(f):
        for g in range(groups):
            relay(ttmp.at[g], 0, f, g, chunks - 1)
            tail = ttmp[g, pl.ds((CHUNK - 2) * SUB, 2 * SUB), :]
            hsend[f * groups + g] = tail.astype(BF16)
            if f:
                head[g, pl.ds((2 + 2 * f) * SUB, 2 * SUB), :] = tail

    tails[0].wait()
    tail_of(1)
    tail_of(2)
    halo = remote(hsend, hrecv, hs_sem, hr_sem, nxt)

    par_cps[0].wait()
    par_cps[1].wait()
    for f in (1, 2):
        for g in range(groups):
            fg = f * groups + g
            for s in range(SUB):
                taps_t[pl.ds(fg * 3 * SUB + s, 3, stride=SUB), :] = taps_n[:, pl.ds(fg * GROUP + s * LANE, LANE)]
    for g in range(groups):
        for s in range(SUB):
            rtm[g, pl.ds(s, modes, stride=SUB), :] = rate_n[:, pl.ds(g * GROUP + s * LANE, LANE)]
        r = rtm[g]
        dtm[g] = jnp.exp(-r)
        d16[g] = jnp.exp(-float(CHUNK) * r)

    def tap(f, g):
        return [taps_t[pl.ds(pl.multiple_of(((f * groups + g) * 3 + j) * SUB, SUB), SUB), :] for j in range(3)]

    def mode(ref, g, m):
        return ref[g, pl.ds(m * SUB, SUB), :]

    def at(t):
        return pl.ds(pl.multiple_of(t * SUB, SUB), SUB)

    def tree(vals):
        vals = list(vals)
        while len(vals) > 1:
            vals = [a + b for a, b in zip(vals[::2], vals[1::2])] + (vals[-1:] if len(vals) % 2 else [])
        return vals[0]

    zero = jnp.zeros((SUB, LANE), F32)

    def states(g):
        d = [mode(dtm, g, m) for m in range(modes)]
        tk, tv = tap(1, g), tap(2, g)
        relay(ktmp, 0, 1, g, 0)
        relay(vtmp, 0, 2, g, 0)
        head[g, pl.ds(0, 2 * SUB), :] = ktmp[pl.ds(0, 2 * SUB), :]
        head[g, pl.ds(2 * SUB, 2 * SUB), :] = vtmp[pl.ds(0, 2 * SUB), :]
        for m in range(modes):
            ztm[g, pl.ds(m * SUB, SUB), :] = zero

        def chunk(c, bufs, spare, carry):
            ahead = jnp.minimum(c + 1, chunks - 1)
            relay(spare[0], 0, 1, g, ahead)
            relay(spare[1], 0, 2, g, ahead)
            k1, k2, v1, v2 = carry
            u = [None] * modes
            for t in range(CHUNK):
                k0, v0 = bufs[0][pl.ds(t * SUB, SUB), :], bufs[1][pl.ds(t * SUB, SUB), :]
                x = (tk[0] * k0 + tk[1] * k1 + tk[2] * k2) * (tv[0] * v0 + tv[1] * v1 + tv[2] * v2)
                if t < 2:
                    x = jnp.where(c == 0, zero, x)
                k1, k2, v1, v2 = k0, k1, v0, v1
                xs[g, at(c * CHUNK + t), :] = x
                u = [x if u[m] is None else d[m] * u[m] + x for m in range(modes)]
            for m in range(modes):
                ends[g, at(c * modes + m), :] = u[m]
                ztm[g, pl.ds(m * SUB, SUB), :] = mode(d16, g, m) * mode(ztm, g, m) + u[m]
            return k1, k2, v1, v2

        def pair(j, carry):
            carry = chunk(2 * j, (ktmp, vtmp), (ktmp2, vtmp2), carry)
            return chunk(2 * j + 1, (ktmp2, vtmp2), (ktmp, vtmp), carry)

        lax.fori_loop(0, chunks // 2, pair, (zero, zero, zero, zero))

    first = p == 0

    def halo_of(f, g):
        both = hrecv[f * groups + g].astype(F32)
        both = jnp.where(first, jnp.zeros_like(both), both)
        return both[:SUB], both[SUB:]

    def edges(g):
        feats = []
        for n, f in enumerate((1, 2)):
            h2, h1 = halo_of(f, g)
            t0, t1, t2 = tap(f, g)
            e0, e1 = head[g, pl.ds(2 * n * SUB, SUB), :], head[g, pl.ds((2 * n + 1) * SUB, SUB), :]
            feats.append((t0 * e0 + t1 * h1 + t2 * h2, t0 * e1 + t1 * e0 + t2 * h1))
        edge[g, pl.ds(0, SUB), :] = feats[0][0] * feats[1][0]
        edge[g, pl.ds(SUB, SUB), :] = feats[0][1] * feats[1][1]

    def stage(g):
        for m in range(modes):
            stg[g, pl.ds(m, SUB, stride=modes), :] = mode(ztm, g, m)
        for s in range(SUB):
            send1[g * SUB + s, pl.ds(0, modes), :] = stg[g, pl.ds(s * modes, modes), :].astype(BF16)
            send1[g * SUB + s, pl.ds(modes, SUB), :] = head[g, pl.ds(s, SUB, stride=SUB), :].astype(BF16)

    def emit(g):
        for s in range(SUB):
            n, to = g * SUB + s, own_by(g, s)

            @pl.when(to == e)
            def _():
                recv1[e] = send1[n]

            @pl.when(to != e)
            def _():
                remote(send1.at[n], recv1.at[e], s1_sem.at[n], r1_sem.at[e], mate(to)).start()

    def emit_all(k, _):
        emit(far_first(k))
        return 0

    half = min(2, groups - 1)
    for idx in range(groups):
        if idx < 2:
            for k in ((0,) if idx == 0 else range(1, groups)):
                for f in (1, 2):
                    in_copy(f, far_first(k)).wait()
        states(far_first(idx))
        stage(far_first(idx))
        if idx == half - 1:
            @pl.when(late)
            def _():
                pl.semaphore_wait(bar, n1 + n2)
                lax.fori_loop(0, half, emit_all, 0)
        elif half <= idx < groups - 1:
            @pl.when(late)
            def _():
                emit(far_first(idx))

    if half:
        @pl.when(jnp.logical_not(late))
        def _():
            pl.semaphore_wait(bar, n1 + n2)
            lax.fori_loop(0, groups - 1, emit_all, 0)
    else:
        pl.semaphore_wait(bar, n1 + n2)
    emit(far_first(groups - 1))

    tails[1].wait()
    tail_of(0)
    halo.start()
    par_cps[2].wait()
    par_cps[3].wait()
    for g in range(groups):
        for s in range(SUB):
            taps_t[pl.ds(g * 3 * SUB + s, 3, stride=SUB), :] = taps_n[:, pl.ds(g * GROUP + s * LANE, LANE)]
            cols = pl.ds(g * GROUP + s * LANE, LANE)
            atm[g, pl.ds(s, modes, stride=SUB), :] = res_n[:, cols] * jnp.sqrt(2.0 * rate_n[:, cols])
    for g in range(groups):
        in_copy(0, g).wait()
        t0, t1, t2 = tap(0, g)

        def gate(c, bufs, spare, carry):
            relay(spare, 0, 0, g, jnp.minimum(c + 1, chunks - 1))
            q1, q2 = carry
            for t in range(CHUNK):
                q0 = bufs[pl.ds(t * SUB, SUB), :]
                qtm[g, at(c * CHUNK + t), :] = t0 * q0 + t1 * q1 + t2 * q2
                q1, q2 = q0, q1
            return q1, q2

        def gates(j, carry):
            return gate(2 * j + 1, ktmp2, ktmp, gate(2 * j, ktmp, ktmp2, carry))

        relay(ktmp, 0, 0, g, 0)
        lax.fori_loop(0, chunks // 2, gates, (zero, zero))

    own_cols = pl.ds(pl.multiple_of(mine * LANE, LANE), LANE)
    own = rate_n[:, own_cols]
    dec_in = jnp.exp(-float(rows) * own)
    dec_out = jnp.exp(-float(rows * n1) * own)
    dec_one, dec_edge = jnp.exp(-own), jnp.exp(-(rows - 2.0) * own)
    own_taps = [taps_n[pl.ds(j, 1), pl.ds(pl.multiple_of(f * channels + mine * LANE, LANE), LANE)]
                for f in (1, 2) for j in range(3)]

    def row(base_row, j):
        return xwork[pl.ds(base_row + j, 1), :]

    def edge_state(heads, tails):
        ends_x = []
        for j in (0, 1):
            t0, t1, t2 = own_taps[3 * j:3 * j + 3]
            e0, e1, h2, h1 = heads[2 * j], heads[2 * j + 1], tails[2 * j], tails[2 * j + 1]
            ends_x.append((t0 * e0 + t1 * h1 + t2 * h2, t0 * e1 + t1 * e0 + t2 * h1))
        x0, x1 = ends_x[0][0] * ends_x[1][0], ends_x[0][1] * ends_x[1][1]
        return dec_edge * (dec_one * x0 + x1)

    run = jnp.zeros((modes, LANE), F32)
    for n in range(n1):
        pre[n] = run

        @pl.when(n != e)
        def _():
            remote(send1.at[n], recv1.at[n], s1_sem.at[n], r1_sem.at[n], mate(n)).wait_recv()

        run = dec_in * run + recv1[n, pl.ds(0, modes), :].astype(F32)
        xwork[pl.ds(n * SUB, SUB), :] = recv1[n, pl.ds(modes, SUB), :].astype(F32)
        if n:
            run = run + edge_state([row(n * SUB, j) for j in range(4)], [row((n - 1) * SUB + 4, j) for j in range(4)])
    rim = [xwork[pl.ds(0, 4), :], xwork[pl.ds((n1 - 1) * SUB + 4, 4), :]]
    send2[1, pl.ds(0, 8), :] = jnp.concatenate(rim, 0).astype(BF16)
    send2[0] = run.astype(BF16)
    for k in range(n2 - 1, 0, -1):
        @pl.when(h + k < n2)
        def _():
            remote(send2, recv2.at[h], s2_sem.at[k], r2_sem.at[h], dev((h + k) * n1 + e)).start()

    power = jnp.ones((modes, LANE), F32)
    for n in range(n1):
        powr[n] = power
        power = power * dec_in

    def local(g):
        d = [mode(dtm, g, m) for m in range(modes)]
        a = [mode(atm, g, m) for m in range(modes)]
        taps = []
        for j in range(CHUNK):
            taps.append(tree(a))
            a = [d[m] * a[m] for m in range(modes)]
        taps[0] = taps[0] + skip_v[pl.ds(g * SUB, SUB), :]

        def body(c, _):
            x = [xs[g, at(c * CHUNK + t), :] for t in range(CHUNK)]
            for t in range(CHUNK):
                base[g, at(c * CHUNK + t), :] = tree([taps[j] * x[t - j] for j in range(t + 1)])
            for m in range(modes):
                ends[g, at(c * modes + m), :] = mode(atm, g, m) * ends[g, at(c * modes + m), :]
            return 0

        lax.fori_loop(0, chunks, body, 0)

    def fix_edge(g):
        x0, x1 = edge[g, pl.ds(0, SUB), :], edge[g, pl.ds(SUB, SUB), :]
        sk = skip_v[pl.ds(g * SUB, SUB), :]
        lead = tree([mode(atm, g, m) * jnp.exp(mode(rtm, g, m)) for m in range(modes)])
        base[g, pl.ds(0, SUB), :] = sk * x0 - x1 * lead
        base[g, pl.ds(SUB, SUB), :] = sk * x1
        for m in range(modes):
            r = mode(rtm, g, m)
            ztm[g, pl.ds(m * SUB, SUB), :] = jnp.exp(r) * x0 + jnp.exp(2.0 * r) * x1

    split = (groups + 1) // 2
    for g in range(split):
        local(g)

    def add_outer(n, carry):
        acc, tails = carry[0], carry[1:]
        remote(send2, recv2.at[n], s2_sem.at[0], r2_sem.at[n], dev(n * n1 + e)).wait_recv()
        xwork[pl.ds(n1 * SUB, SUB), :] = recv2[n, 1, pl.ds(0, 8), :].astype(F32)
        both = [row(n1 * SUB, j) for j in range(8)]
        whole = recv2[n, 0].astype(F32) + last_power * edge_state(both[:4], tails)
        return (dec_out * acc + whole, *both[4:])

    last_power = powr[n1 - 1]
    none = jnp.zeros((1, LANE), F32)
    done = lax.fori_loop(0, h, add_outer, (jnp.zeros((modes, LANE), F32), none, none, none, none))
    carried = done[0]
    after = dec_in * carried + edge_state([row(0, j) for j in range(4)], done[1:])
    send3[0] = carried.astype(BF16)
    for n in range(1, n1):
        send3[n] = (pre[n] + powr[n - 1] * after).astype(BF16)
    recv3[mine] = send3[e]
    for n in list(ring_order())[::-1]:
        remote(send3.at[n], recv3.at[mine], s3_sem.at[n], r3_sem.at[mine], mate(n)).start()
    for g in range(split, groups):
        local(g)
    halo.wait_recv()
    for g in range(groups):
        edges(g)
        fix_edge(g)
    for g in range(groups):
        h2, h1 = halo_of(0, g)
        t0, t1, t2 = tap(0, g)
        qtm[g, pl.ds(0, SUB), :] = qtm[g, pl.ds(0, SUB), :] + (t1 * h1 + t2 * h2)
        qtm[g, pl.ds(SUB, SUB), :] = qtm[g, pl.ds(SUB, SUB), :] + t2 * h1

    def drained():
        halo.wait_send()

        def drain(n, _):
            @pl.when(n != mine)
            def _():
                remote(send1.at[n], send1.at[n], s1_sem.at[n], s1_sem.at[n], nxt).wait_send()

            @pl.when(n != e)
            def _():
                remote(send3.at[n], send3.at[n], s3_sem.at[n], s3_sem.at[n], nxt).wait_send()

            return 0

        lax.fori_loop(0, n1, drain, 0)
        for k in range(1, n2):
            @pl.when(h + k < n2)
            def _():
                remote(send2, send2, s2_sem.at[k], s2_sem.at[k], nxt).wait_send()

    for idx in range(groups - 1, -1, -1):
        g = far_first(idx)
        for s in range(SUB):
            n, src = g * SUB + s, own_by(g, s)

            @pl.when(src != e)
            def _():
                remote(send3.at[n], recv3.at[n], s3_sem.at[n], r3_sem.at[n], mate(src)).wait_recv()

            ctm[g, pl.ds(s, modes, stride=SUB), :] = recv3[n].astype(F32)
        d = [mode(dtm, g, m) for m in range(modes)]
        init = tuple(mode(atm, g, m) * (mode(ctm, g, m) + mode(ztm, g, m)) for m in range(modes))

        def apply(c, buf, carry):
            s = list(carry)
            for t in range(CHUNK):
                s = [d[m] * s[m] for m in range(modes)]
                here = at(c * CHUNK + t)
                buf[pl.ds(t * SUB, SUB), :] = qtm[g, here, :] * (base[g, here, :] + tree(s))
            for w in range(SUB):
                v = buf[pl.ds(w, CHUNK, stride=SUB), :].astype(BF16)
                cols = pl.ds(pl.multiple_of(g * GROUP + w * LANE, LANE), LANE)
                out[pl.ds(pl.multiple_of(c * CHUNK, CHUNK), CHUNK), cols] = v
            return tuple(s[m] + ends[g, at(c * modes + m), :] for m in range(modes))

        def applies(j, carry):
            return apply(2 * j + 1, ytmp2, apply(2 * j, ytmp, carry))

        lax.fori_loop(0, chunks // 2, applies, init)
        if idx == min(1, groups - 1):
            drained()


def solution(mesh):
    outer_n, inner_n = mesh.shape["outer"], mesh.shape["inner"]

    def on_device(projected, short_taps, rates, residues, skip_gain):
        rows, width = projected.shape
        channels, modes = rates.shape
        groups = channels // GROUP
        n1 = channels // LANE
        n2 = outer_n * inner_n // n1
        any_spec = pl.BlockSpec(memory_space=pl.ANY)
        dma = pltpu.SemaphoreType.DMA
        tm = pltpu.VMEM((groups, rows * SUB, LANE), F32)
        pm = pltpu.VMEM((groups, modes * SUB, LANE), F32)
        tmp = pltpu.VMEM((CHUNK * SUB, LANE), F32)
        msg = pltpu.VMEM((n1, modes, LANE), BF16)
        first_msg = pltpu.VMEM((n1, modes + SUB, LANE), BF16)
        return pl.pallas_call(
            functools.partial(kernel, (outer_n, inner_n, rows, channels, modes)),
            out_shape=pltpu.VMEM((rows, channels), BF16),
            in_specs=[any_spec] * 5,
            out_specs=pl.BlockSpec(memory_space=pltpu.VMEM),
            scratch_shapes=[
                pltpu.VMEM((rows, width), BF16), tmp, tmp, tmp, tmp,
                pltpu.VMEM((groups, CHUNK * SUB, LANE), F32), tm, tm, tm,
                pltpu.VMEM((3, width), F32), pltpu.VMEM((modes, channels), F32), pltpu.VMEM((modes, channels), F32),
                pltpu.VMEM((groups * SUB, LANE), F32), pltpu.VMEM((3 * 3 * groups * SUB, LANE), F32),
                pm, pm, pm, pm, pm,
                pltpu.VMEM((groups, rows // CHUNK * modes * SUB, LANE), F32),
                pltpu.VMEM((groups, 2 * SUB, LANE), F32), pltpu.VMEM((groups, 8 * SUB, LANE), F32),
                pm, pm,
                pltpu.VMEM((n1, modes, LANE), F32), pltpu.VMEM((n1, modes, LANE), F32),
                pltpu.VMEM((3 * groups, 2 * SUB, LANE), BF16), pltpu.VMEM((3 * groups, 2 * SUB, LANE), BF16),
                pltpu.VMEM(((n1 + 1) * SUB, LANE), F32), first_msg, first_msg,
                pltpu.VMEM((2, modes, LANE), BF16), pltpu.VMEM((n2, 2, modes, LANE), BF16), msg, msg,
                tmp, tmp,
                dma((3 * groups + 2,)), dma((4,)), dma, dma,
                dma((n1,)), dma((n1,)), dma((n2,)), dma((n2,)), dma((n1,)), dma((n1,)),
            ],
            compiler_params=pltpu.CompilerParams(collective_id=0, has_side_effects=True,
                                                 vmem_limit_bytes=60 * 1024 * 1024),
            name="modal_scan",
        )(projected, short_taps, rates.T, residues.T, skip_gain.reshape(groups * SUB, LANE))

    return jax.shard_map(
        on_device, mesh=mesh,
        in_specs=(P(("outer", "inner"), None), P(), P(), P(), P()),
        out_specs=P(("outer", "inner"), None), check_vma=False,
    )
```

```python
import functools

import jax
import jax.numpy as jnp
from jax import lax
from jax.experimental import pallas as pl
from jax.experimental.pallas import tpu as pltpu
from jax.sharding import PartitionSpec as P

MESH = pl.DeviceIdType.MESH
F32 = jnp.float32
BF16 = jnp.bfloat16
SUB = 8
LANE = 128
GROUP = SUB * LANE
CHUNK = 16
RING = 8


def kernel(dims, proj, taps_in, rates_in, resid_in, skip_in, out, raw, ktmp, vtmp, ktmp2, vtmp2, ttmp, qtm, xs, base, taps_n,
           rate_n, res_n, skip_v, taps_t, rtm, dtm, d16, atm, ztm, ends, edge, head, stg, ctm, pre, powr, hsend, hrecv, xwork,
           send1, recv1, send2, recv2, send3, recv3, ytmp, ytmp2, in_sem, par_sem, hs_sem, hr_sem,
           s1_sem, r1_sem, s2_sem, r2_sem, s3_sem, r3_sem):
    outer_n, inner_n, rows, channels, modes = dims
    groups = channels // GROUP
    chunks = rows // CHUNK
    n1 = channels // LANE
    total = outer_n * inner_n
    n2 = total // n1
    last = rows - CHUNK
    p = lax.axis_index("outer") * inner_n + lax.axis_index("inner")
    e = lax.rem(p, n1)
    h = p // n1
    z = lax.rem(e, RING)
    hi = e // RING
    zpg = RING // groups
    late = z >= RING // 2
    mine = (z // zpg) * SUB + hi * zpg + lax.rem(z, zpg)

    def far_first(idx):
        if groups == 1:
            return 0
        odd = lax.rem(z, 2)
        off = (2, 1 + 2 * odd, 3 - 2 * odd, 0)
        step = off[idx] if isinstance(idx, int) else jnp.where(
            idx == 0, off[0], jnp.where(idx == 1, off[1], jnp.where(idx == 2, off[2], off[3])))
        return lax.rem(z // zpg + step, groups)

    def own_by(g, s):
        return (s // zpg) * RING + zpg * g + s % zpg

    def dev(r):
        return (r // inner_n, lax.rem(r, inner_n))

    def mate(n):
        return dev(h * n1 + n)

    def ring_order(order=(4, 3, 5, 2, 6, 1, 7, 0)):
        for dz in order:
            for hi in range(n1 // RING):
                if dz or hi:
                    yield lax.rem(e // RING + hi, n1 // RING) * RING + lax.rem(lax.rem(e, RING) + dz, RING)

    def remote(src, dst, ssem, rsem, to):
        return pltpu.make_async_remote_copy(src_ref=src, dst_ref=dst, send_sem=ssem, recv_sem=rsem, device_id=to,
                                            device_id_type=MESH)

    bar = pltpu.get_barrier_semaphore()
    nxt, prv = dev(lax.rem(p + 1, total)), dev(lax.rem(p + total - 1, total))
    for n in ring_order():
        pl.semaphore_signal(bar, inc=1, device_id=mate(n), device_id_type=MESH)
    for to in (nxt, prv):
        pl.semaphore_signal(bar, inc=1, device_id=to, device_id_type=MESH)
    for k in range(1, n2):
        pl.semaphore_signal(bar, inc=1, device_id=dev(lax.rem(h + k, n2) * n1 + e), device_id_type=MESH)

    kv = pl.ds(channels, 2 * channels)
    tails = [pltpu.make_async_copy(proj.at[pl.ds(last, CHUNK), c], raw.at[pl.ds(last, CHUNK), c], in_sem.at[3 * groups + n])
             for n, c in enumerate((kv, pl.ds(0, channels)))]
    tails[0].start()
    par_cps = [pltpu.make_async_copy(a, b, par_sem.at[n]) for n, (a, b) in enumerate(
        ((rates_in, rate_n), (taps_in, taps_n), (resid_in, res_n), (skip_in, skip_v)))]
    par_cps[0].start()
    par_cps[1].start()

    def in_copy(f, g):
        cols = pl.ds(pl.multiple_of((f * groups + g) * GROUP, GROUP), GROUP)
        return pltpu.make_async_copy(proj.at[pl.ds(0, last), cols], raw.at[pl.ds(0, last), cols],
                                     in_sem.at[f * groups + g])

    for idx in range(groups):
        in_copy(1, far_first(idx)).start()
        in_copy(2, far_first(idx)).start()
    par_cps[2].start()
    par_cps[3].start()
    tails[1].start()
    for g in range(groups):
        in_copy(0, g).start()

    def relay(dst, row, f, g, c):
        for s in range(SUB):
            col = pl.multiple_of((f * groups + g) * GROUP + s * LANE, LANE)
            v = raw[pl.ds(pl.multiple_of(c * CHUNK, CHUNK), CHUNK), pl.ds(col, LANE)].astype(F32)
            dst[pl.ds(row + s, CHUNK, stride=SUB), :] = v

    def tail_of(f):
        for g in range(groups):
            relay(ttmp.at[g], 0, f, g, chunks - 1)
            tail = ttmp[g, pl.ds((CHUNK - 2) * SUB, 2 * SUB), :]
            hsend[f * groups + g] = tail.astype(BF16)
            if f:
                head[g, pl.ds((2 + 2 * f) * SUB, 2 * SUB), :] = tail

    tails[0].wait()
    tail_of(1)
    tail_of(2)
    halo = remote(hsend, hrecv, hs_sem, hr_sem, nxt)

    par_cps[0].wait()
    par_cps[1].wait()
    for f in (1, 2):
        for g in range(groups):
            fg = f * groups + g
            for s in range(SUB):
                taps_t[pl.ds(fg * 3 * SUB + s, 3, stride=SUB), :] = taps_n[:, pl.ds(fg * GROUP + s * LANE, LANE)]
    for g in range(groups):
        for s in range(SUB):
            rtm[g, pl.ds(s, modes, stride=SUB), :] = rate_n[:, pl.ds(g * GROUP + s * LANE, LANE)]
        r = rtm[g]
        dtm[g] = jnp.exp(-r)
        d16[g] = jnp.exp(-float(CHUNK) * r)

    def tap(f, g):
        return [taps_t[pl.ds(pl.multiple_of(((f * groups + g) * 3 + j) * SUB, SUB), SUB), :] for j in range(3)]

    def mode(ref, g, m):
        return ref[g, pl.ds(m * SUB, SUB), :]

    def at(t):
        return pl.ds(pl.multiple_of(t * SUB, SUB), SUB)

    def tree(vals):
        vals = list(vals)
        while len(vals) > 1:
            vals = [a + b for a, b in zip(vals[::2], vals[1::2])] + (vals[-1:] if len(vals) % 2 else [])
        return vals[0]

    zero = jnp.zeros((SUB, LANE), F32)

    def states(g):
        d = [mode(dtm, g, m) for m in range(modes)]
        tk, tv = tap(1, g), tap(2, g)
        relay(ktmp, 0, 1, g, 0)
        relay(vtmp, 0, 2, g, 0)
        head[g, pl.ds(0, 2 * SUB), :] = ktmp[pl.ds(0, 2 * SUB), :]
        head[g, pl.ds(2 * SUB, 2 * SUB), :] = vtmp[pl.ds(0, 2 * SUB), :]
        for m in range(modes):
            ztm[g, pl.ds(m * SUB, SUB), :] = zero

        def chunk(c, bufs, spare, carry):
            ahead = jnp.minimum(c + 1, chunks - 1)
            relay(spare[0], 0, 1, g, ahead)
            relay(spare[1], 0, 2, g, ahead)
            k1, k2, v1, v2 = carry
            u = [None] * modes
            for t in range(CHUNK):
                k0, v0 = bufs[0][pl.ds(t * SUB, SUB), :], bufs[1][pl.ds(t * SUB, SUB), :]
                x = (tk[0] * k0 + tk[1] * k1 + tk[2] * k2) * (tv[0] * v0 + tv[1] * v1 + tv[2] * v2)
                if t < 2:
                    x = jnp.where(c == 0, zero, x)
                k1, k2, v1, v2 = k0, k1, v0, v1
                xs[g, at(c * CHUNK + t), :] = x
                u = [x if u[m] is None else d[m] * u[m] + x for m in range(modes)]
            for m in range(modes):
                ends[g, at(c * modes + m), :] = u[m]
                ztm[g, pl.ds(m * SUB, SUB), :] = mode(d16, g, m) * mode(ztm, g, m) + u[m]
            return k1, k2, v1, v2

        def pair(j, carry):
            carry = chunk(2 * j, (ktmp, vtmp), (ktmp2, vtmp2), carry)
            return chunk(2 * j + 1, (ktmp2, vtmp2), (ktmp, vtmp), carry)

        lax.fori_loop(0, chunks // 2, pair, (zero, zero, zero, zero))

    first = p == 0

    def halo_of(f, g):
        both = hrecv[f * groups + g].astype(F32)
        both = jnp.where(first, jnp.zeros_like(both), both)
        return both[:SUB], both[SUB:]

    def edges(g):
        feats = []
        for n, f in enumerate((1, 2)):
            h2, h1 = halo_of(f, g)
            t0, t1, t2 = tap(f, g)
            e0, e1 = head[g, pl.ds(2 * n * SUB, SUB), :], head[g, pl.ds((2 * n + 1) * SUB, SUB), :]
            feats.append((t0 * e0 + t1 * h1 + t2 * h2, t0 * e1 + t1 * e0 + t2 * h1))
        edge[g, pl.ds(0, SUB), :] = feats[0][0] * feats[1][0]
        edge[g, pl.ds(SUB, SUB), :] = feats[0][1] * feats[1][1]

    def stage(g):
        for m in range(modes):
            stg[g, pl.ds(m, SUB, stride=modes), :] = mode(ztm, g, m)
        for s in range(SUB):
            send1[g * SUB + s, pl.ds(0, modes), :] = stg[g, pl.ds(s * modes, modes), :].astype(BF16)
            send1[g * SUB + s, pl.ds(modes, SUB), :] = head[g, pl.ds(s, SUB, stride=SUB), :].astype(BF16)

    def emit(g):
        for s in range(SUB):
            n, to = g * SUB + s, own_by(g, s)

            @pl.when(to == e)
            def _():
                recv1[e] = send1[n]

            @pl.when(to != e)
            def _():
                remote(send1.at[n], recv1.at[e], s1_sem.at[n], r1_sem.at[e], mate(to)).start()

    def emit_all(k, _):
        emit(far_first(k))
        return 0

    half = min(2, groups - 1)
    for idx in range(groups):
        if idx < 2:
            for k in ((0,) if idx == 0 else range(1, groups)):
                for f in (1, 2):
                    in_copy(f, far_first(k)).wait()
        states(far_first(idx))
        stage(far_first(idx))
        if idx == half - 1:
            @pl.when(late)
            def _():
                pl.semaphore_wait(bar, n1 + n2)
                lax.fori_loop(0, half, emit_all, 0)
        elif half <= idx < groups - 1:
            @pl.when(late)
            def _():
                emit(far_first(idx))

    if half:
        @pl.when(jnp.logical_not(late))
        def _():
            pl.semaphore_wait(bar, n1 + n2)
            lax.fori_loop(0, groups - 1, emit_all, 0)
    else:
        pl.semaphore_wait(bar, n1 + n2)
    emit(far_first(groups - 1))

    tails[1].wait()
    tail_of(0)
    par_cps[2].wait()
    par_cps[3].wait()
    for g in range(groups):
        for s in range(SUB):
            taps_t[pl.ds(g * 3 * SUB + s, 3, stride=SUB), :] = taps_n[:, pl.ds(g * GROUP + s * LANE, LANE)]
            cols = pl.ds(g * GROUP + s * LANE, LANE)
            atm[g, pl.ds(s, modes, stride=SUB), :] = res_n[:, cols] * jnp.sqrt(2.0 * rate_n[:, cols])
    for g in range(groups):
        in_copy(0, g).wait()
        t0, t1, t2 = tap(0, g)

        def gate(c, bufs, spare, carry):
            relay(spare, 0, 0, g, jnp.minimum(c + 1, chunks - 1))
            q1, q2 = carry
            for t in range(CHUNK):
                q0 = bufs[pl.ds(t * SUB, SUB), :]
                qtm[g, at(c * CHUNK + t), :] = t0 * q0 + t1 * q1 + t2 * q2
                q1, q2 = q0, q1
            return q1, q2

        def gates(j, carry):
            return gate(2 * j + 1, ktmp2, ktmp, gate(2 * j, ktmp, ktmp2, carry))

        relay(ktmp, 0, 0, g, 0)
        lax.fori_loop(0, chunks // 2, gates, (zero, zero))

    own_cols = pl.ds(pl.multiple_of(mine * LANE, LANE), LANE)
    own = rate_n[:, own_cols]
    dec_in = jnp.exp(-float(rows) * own)
    dec_out = jnp.exp(-float(rows * n1) * own)
    dec_one, dec_edge = jnp.exp(-own), jnp.exp(-(rows - 2.0) * own)
    own_taps = [taps_n[pl.ds(j, 1), pl.ds(pl.multiple_of(f * channels + mine * LANE, LANE), LANE)]
                for f in (1, 2) for j in range(3)]

    def row(base_row, j):
        return xwork[pl.ds(base_row + j, 1), :]

    def edge_state(heads, tails):
        ends_x = []
        for j in (0, 1):
            t0, t1, t2 = own_taps[3 * j:3 * j + 3]
            e0, e1, h2, h1 = heads[2 * j], heads[2 * j + 1], tails[2 * j], tails[2 * j + 1]
            ends_x.append((t0 * e0 + t1 * h1 + t2 * h2, t0 * e1 + t1 * e0 + t2 * h1))
        x0, x1 = ends_x[0][0] * ends_x[1][0], ends_x[0][1] * ends_x[1][1]
        return dec_edge * (dec_one * x0 + x1)

    run = jnp.zeros((modes, LANE), F32)
    for n in range(n1):
        pre[n] = run

        @pl.when(n != e)
        def _():
            remote(send1.at[n], recv1.at[n], s1_sem.at[n], r1_sem.at[n], mate(n)).wait_recv()

        run = dec_in * run + recv1[n, pl.ds(0, modes), :].astype(F32)
        xwork[pl.ds(n * SUB, SUB), :] = recv1[n, pl.ds(modes, SUB), :].astype(F32)
        if n:
            run = run + edge_state([row(n * SUB, j) for j in range(4)], [row((n - 1) * SUB + 4, j) for j in range(4)])
    rim = [xwork[pl.ds(0, 4), :], xwork[pl.ds((n1 - 1) * SUB + 4, 4), :]]
    send2[1, pl.ds(0, 8), :] = jnp.concatenate(rim, 0).astype(BF16)
    send2[0] = run.astype(BF16)
    for k in range(n2 - 1, 0, -1):
        @pl.when(h + k < n2)
        def _():
            remote(send2, recv2.at[h], s2_sem.at[k], r2_sem.at[h], dev((h + k) * n1 + e)).start()

    halo.start()

    power = jnp.ones((modes, LANE), F32)
    for n in range(n1):
        powr[n] = power
        power = power * dec_in

    def local(g):
        d = [mode(dtm, g, m) for m in range(modes)]
        a = [mode(atm, g, m) for m in range(modes)]
        taps = []
        for j in range(CHUNK):
            taps.append(tree(a))
            a = [d[m] * a[m] for m in range(modes)]
        taps[0] = taps[0] + skip_v[pl.ds(g * SUB, SUB), :]

        def body(c, _):
            x = [xs[g, at(c * CHUNK + t), :] for t in range(CHUNK)]
            for t in range(CHUNK):
                base[g, at(c * CHUNK + t), :] = tree([taps[j] * x[t - j] for j in range(t + 1)])
            for m in range(modes):
                ends[g, at(c * modes + m), :] = mode(atm, g, m) * ends[g, at(c * modes + m), :]
            return 0

        lax.fori_loop(0, chunks, body, 0)

    def fix_edge(g):
        x0, x1 = edge[g, pl.ds(0, SUB), :], edge[g, pl.ds(SUB, SUB), :]
        sk = skip_v[pl.ds(g * SUB, SUB), :]
        lead = tree([mode(atm, g, m) * jnp.exp(mode(rtm, g, m)) for m in range(modes)])
        base[g, pl.ds(0, SUB), :] = sk * x0 - x1 * lead
        base[g, pl.ds(SUB, SUB), :] = sk * x1
        for m in range(modes):
            r = mode(rtm, g, m)
            ztm[g, pl.ds(m * SUB, SUB), :] = jnp.exp(r) * x0 + jnp.exp(2.0 * r) * x1

    split = (groups + 1) // 2
    for g in range(split):
        local(g)

    def add_outer(n, carry):
        acc, tails = carry[0], carry[1:]
        remote(send2, recv2.at[n], s2_sem.at[0], r2_sem.at[n], dev(n * n1 + e)).wait_recv()
        xwork[pl.ds(n1 * SUB, SUB), :] = recv2[n, 1, pl.ds(0, 8), :].astype(F32)
        both = [row(n1 * SUB, j) for j in range(8)]
        whole = recv2[n, 0].astype(F32) + last_power * edge_state(both[:4], tails)
        return (dec_out * acc + whole, *both[4:])

    last_power = powr[n1 - 1]
    none = jnp.zeros((1, LANE), F32)
    done = lax.fori_loop(0, h, add_outer, (jnp.zeros((modes, LANE), F32), none, none, none, none))
    carried = done[0]
    after = dec_in * carried + edge_state([row(0, j) for j in range(4)], done[1:])
    send3[0] = carried.astype(BF16)
    for n in range(1, n1):
        send3[n] = (pre[n] + powr[n - 1] * after).astype(BF16)
    recv3[mine] = send3[e]
    for n in ring_order((0, 1, 7, 2, 6, 4, 3, 5)):
        remote(send3.at[n], recv3.at[mine], s3_sem.at[n], r3_sem.at[mine], mate(n)).start()
    for g in range(split, groups):
        local(g)
    halo.wait_recv()
    for g in range(groups):
        edges(g)
        fix_edge(g)
    for g in range(groups):
        h2, h1 = halo_of(0, g)
        t0, t1, t2 = tap(0, g)
        qtm[g, pl.ds(0, SUB), :] = qtm[g, pl.ds(0, SUB), :] + (t1 * h1 + t2 * h2)
        qtm[g, pl.ds(SUB, SUB), :] = qtm[g, pl.ds(SUB, SUB), :] + t2 * h1

    def drained():
        halo.wait_send()

        def drain(n, _):
            @pl.when(n != mine)
            def _():
                remote(send1.at[n], send1.at[n], s1_sem.at[n], s1_sem.at[n], nxt).wait_send()

            @pl.when(n != e)
            def _():
                remote(send3.at[n], send3.at[n], s3_sem.at[n], s3_sem.at[n], nxt).wait_send()

            return 0

        lax.fori_loop(0, n1, drain, 0)
        for k in range(1, n2):
            @pl.when(h + k < n2)
            def _():
                remote(send2, send2, s2_sem.at[k], s2_sem.at[k], nxt).wait_send()

    for idx in range(groups - 1, -1, -1):
        g = far_first(idx)
        for s in range(SUB):
            n, src = g * SUB + s, own_by(g, s)

            @pl.when(src != e)
            def _():
                remote(send3.at[n], recv3.at[n], s3_sem.at[n], r3_sem.at[n], mate(src)).wait_recv()

            ctm[g, pl.ds(s, modes, stride=SUB), :] = recv3[n].astype(F32)
        d = [mode(dtm, g, m) for m in range(modes)]
        init = tuple(mode(atm, g, m) * (mode(ctm, g, m) + mode(ztm, g, m)) for m in range(modes))

        def apply(c, buf, carry):
            s = list(carry)
            for t in range(CHUNK):
                s = [d[m] * s[m] for m in range(modes)]
                here = at(c * CHUNK + t)
                buf[pl.ds(t * SUB, SUB), :] = qtm[g, here, :] * (base[g, here, :] + tree(s))
            for w in range(SUB):
                v = buf[pl.ds(w, CHUNK, stride=SUB), :].astype(BF16)
                cols = pl.ds(pl.multiple_of(g * GROUP + w * LANE, LANE), LANE)
                out[pl.ds(pl.multiple_of(c * CHUNK, CHUNK), CHUNK), cols] = v
            return tuple(s[m] + ends[g, at(c * modes + m), :] for m in range(modes))

        def applies(j, carry):
            return apply(2 * j + 1, ytmp2, apply(2 * j, ytmp, carry))

        lax.fori_loop(0, chunks // 2, applies, init)
        if idx == min(1, groups - 1):
            drained()


def solution(mesh):
    outer_n, inner_n = mesh.shape["outer"], mesh.shape["inner"]

    def on_device(projected, short_taps, rates, residues, skip_gain):
        rows, width = projected.shape
        channels, modes = rates.shape
        groups = channels // GROUP
        n1 = channels // LANE
        n2 = outer_n * inner_n // n1
        any_spec = pl.BlockSpec(memory_space=pl.ANY)
        dma = pltpu.SemaphoreType.DMA
        tm = pltpu.VMEM((groups, rows * SUB, LANE), F32)
        pm = pltpu.VMEM((groups, modes * SUB, LANE), F32)
        tmp = pltpu.VMEM((CHUNK * SUB, LANE), F32)
        msg = pltpu.VMEM((n1, modes, LANE), BF16)
        first_msg = pltpu.VMEM((n1, modes + SUB, LANE), BF16)
        return pl.pallas_call(
            functools.partial(kernel, (outer_n, inner_n, rows, channels, modes)),
            out_shape=pltpu.VMEM((rows, channels), BF16),
            in_specs=[any_spec] * 5,
            out_specs=pl.BlockSpec(memory_space=pltpu.VMEM),
            scratch_shapes=[
                pltpu.VMEM((rows, width), BF16), tmp, tmp, tmp, tmp,
                pltpu.VMEM((groups, CHUNK * SUB, LANE), F32), tm, tm, tm,
                pltpu.VMEM((3, width), F32), pltpu.VMEM((modes, channels), F32), pltpu.VMEM((modes, channels), F32),
                pltpu.VMEM((groups * SUB, LANE), F32), pltpu.VMEM((3 * 3 * groups * SUB, LANE), F32),
                pm, pm, pm, pm, pm,
                pltpu.VMEM((groups, rows // CHUNK * modes * SUB, LANE), F32),
                pltpu.VMEM((groups, 2 * SUB, LANE), F32), pltpu.VMEM((groups, 8 * SUB, LANE), F32),
                pm, pm,
                pltpu.VMEM((n1, modes, LANE), F32), pltpu.VMEM((n1, modes, LANE), F32),
                pltpu.VMEM((3 * groups, 2 * SUB, LANE), BF16), pltpu.VMEM((3 * groups, 2 * SUB, LANE), BF16),
                pltpu.VMEM(((n1 + 1) * SUB, LANE), F32), first_msg, first_msg,
                pltpu.VMEM((2, modes, LANE), BF16), pltpu.VMEM((n2, 2, modes, LANE), BF16), msg, msg,
                tmp, tmp,
                dma((3 * groups + 2,)), dma((4,)), dma, dma,
                dma((n1,)), dma((n1,)), dma((n2,)), dma((n2,)), dma((n1,)), dma((n1,)),
            ],
            compiler_params=pltpu.CompilerParams(collective_id=0, has_side_effects=True,
                                                 vmem_limit_bytes=60 * 1024 * 1024),
            name="modal_scan",
        )(projected, short_taps, rates.T, residues.T, skip_gain.reshape(groups * SUB, LANE))

    return jax.shard_map(
        on_device, mesh=mesh,
        in_specs=(P(("outer", "inner"), None), P(), P(), P(), P()),
        out_specs=P(("outer", "inner"), None), check_vma=False,
    )
```
